32 devices in a mesh: blk: 8 (over z, y), tm: 4 (over x, core).
Axes of the slice: x: 2, y: 2, z: 4, core: 2. Of those that a mesh axis runs over, the one named last changes fastest.
Arguments:
- solution: float32 [512, 128, 1024], P('blk', 'tm'), may hold values from -6 to 6
- residual: float32 [512, 128, 1024], P('blk', 'tm'), may hold values from -12 to 12
- direction: float32 [512, 128, 1024], P('blk', 'tm'), may hold values from -6 to 6
- noise_var: float32 [512, 128, 1024], P('blk', 'tm'), may hold values from 0.5 to 2
- legendre: bfloat16 [512, 512, 512], P('blk', 'tm'), may hold values from -0.25 to 0.25
- temporal: float32 [512, 128, 128], P('tm'), may hold values from -3 to 3.5, as said below
- order_table: int32 [512], replicated, may hold values from 0 to 511, as said below
Outputs:
- solution_new: float32 [512, 128, 1024], P('blk', 'tm')
- residual_new: float32 [512, 128, 1024], P('blk', 'tm')
- direction_new: float32 [512, 128, 1024], P('blk', 'tm')
The draws below stay inside these ranges and needn't reach their ends.
Inputs may be any that keep to these rules, and one draw needn't show every extreme that they name: `order_table`: each value 0 to 511 appears once. In each aligned block of 64 entries, entry 32 + k equals 511 minus entry k, so each block holds pairs of orders m and 511 - m. `temporal`: each matrix is symmetric and positive definite.
All inputs are finite; a program needn't handle non-finite values.
Results may differ from the reference program's by a relative error of at most 0.0048.
Values may be sent and summed in bfloat16 or wider, within the bound.
No kernel may reach another device: no remote copies, remote signals or barrier semaphores. Data moves between devices by JAX's collectives and lax.ppermute only.
A program may use at most 192 MiB of HBM per device.

```python
import math
import jax
import jax.numpy as jnp
from jax import lax

LAT = 512
LON = 1024
DEGREES = 512
TIME = 128
ORD_DEV = 64


def draw_residual(key, part):
    cycles = jnp.arange(LAT, dtype=jnp.int32).astype(jnp.float32)
    scaling_factor = 1.0 + 2.0 * cycles / (LAT - 1)
    values = jnp.clip(jax.random.normal(key, (LAT, TIME, LON), jnp.float32), -4.0, 4.0)
    return values * scaling_factor[:, None, None]


def draw_temporal(key, part):
    limit = math.sqrt(3.0)
    factors = jax.random.uniform(jax.random.fold_in(key, 11), (DEGREES, TIME, TIME), jnp.float32, -limit, limit) / math.sqrt(TIME)
    gram = jnp.einsum('ltk,luk->ltu', factors, factors)
    return gram + 0.5 * jnp.eye(TIME, dtype=jnp.float32)[None, :, :]


def draw_order_table(key, part):
    pairs = jax.random.permutation(jax.random.fold_in(key, 7), DEGREES // 2).astype(jnp.int32)
    pairs = pairs.reshape(DEGREES // ORD_DEV, ORD_DEV // 2)
    return jnp.concatenate([pairs, DEGREES - 1 - pairs], axis=1).reshape(DEGREES).astype(jnp.int32)


def block_levels(own_key, extent, cuts, least, top_value):
    gain = 1.0
    for position, parts in cuts:
        steps = jax.random.uniform(jax.random.fold_in(jax.random.fold_in(own_key, 6), position), (parts,), jnp.float32, least / len(cuts), top_value / len(cuts))
        gain = gain * jnp.repeat(jnp.exp(steps), extent[position] // parts).reshape((-1,) + (1,) * (len(extent) - 1 - position))
    return gain


def bell_draw(stream_key, dims, deviation, most, shards=(), held_as=jnp.bfloat16):
    values = deviation * jax.random.normal(stream_key, dims, jnp.float32)
    if shards:
        values = values * block_levels(stream_key, dims, shards, -0.22, 0.18)
    return jnp.clip(values, -most, most).astype(held_as)


def setup_inputs(seed: int = 0) -> dict:
    arg_keys = jax.random.split(jax.random.key(seed), 8)
    return {
        "solution": bell_draw(arg_keys[0], (LAT, TIME, LON), 1.0, 6.0, ((0, 8), (1, 4)), jnp.float32),
        "residual": draw_residual(jax.random.fold_in(arg_keys[7], 71), 0),
        "direction": bell_draw(arg_keys[2], (LAT, TIME, LON), 1.0, 6.0, ((0, 8), (1, 4)), jnp.float32),
        "noise_var": jnp.clip(jnp.exp(math.log(2.0) - 1.3862944 * jax.random.uniform(arg_keys[3], (LAT, TIME, LON), jnp.float32) ** block_levels(arg_keys[3], (LAT, TIME, LON), ((0, 8), (1, 4)), -0.2, 0.2)), 0.5, 2.0),
        "legendre": bell_draw(arg_keys[4], (DEGREES, DEGREES, LAT), LAT ** -0.5, 0.25, ((0, 8), (1, 4))),
        "temporal": draw_temporal(jax.random.fold_in(arg_keys[7], 71), 0),
        "order_table": draw_order_table(jax.random.fold_in(arg_keys[7], 71), 0),
    }


def trig_table(orders, length):
    points = jnp.arange(length, dtype=jnp.int32)
    phases = points[:, None] * orders.astype(jnp.int32)[None, :] % length
    angles = phases.astype(jnp.float32) * (2.0 * math.pi / length)
    scaling_factor = 1.0 / math.sqrt(length / 2.0)
    stacked = jnp.stack([jnp.cos(angles), jnp.sin(angles)], axis=-1) * scaling_factor
    return stacked.reshape(length, 2 * orders.shape[0])

def reference(solution, residual, direction, noise_var, legendre, temporal, order_table):
    lookup_table = trig_table(order_table, LON)
    spectra = jnp.dot(direction.reshape(LAT * TIME, LON), lookup_table, precision=lax.Precision.HIGHEST).astype(jnp.bfloat16)
    spectra = spectra.reshape(LAT, TIME, DEGREES, 2).transpose(2, 0, 1, 3).reshape(DEGREES, LAT, TIME * 2)
    degrees = jnp.arange(DEGREES, dtype=jnp.int32)

    def per_order(items):
        rows, order, values = items
        mask_applied = jnp.where((degrees >= order)[:, None], rows, jnp.zeros_like(rows))
        coeffs = jnp.dot(mask_applied, values, preferred_element_type=jnp.float32).reshape(DEGREES, TIME, 2)
        mixed = jnp.einsum('ltu,luc->ltc', temporal, coeffs, precision=lax.Precision.HIGHEST).astype(jnp.bfloat16)
        return jnp.dot(mask_applied.T, mixed.reshape(DEGREES, TIME * 2), preferred_element_type=jnp.float32)
    grids = lax.map(per_order, (legendre, order_table, spectra))
    grids = grids.reshape(DEGREES, LAT, TIME, 2).transpose(1, 2, 0, 3).reshape(LAT * TIME, 2 * DEGREES)
    harmonic_synthesis = jnp.dot(grids, lookup_table.T, precision=lax.Precision.HIGHEST).reshape(LAT, TIME, LON)
    product = harmonic_synthesis + noise_var * direction
    norm_now = jnp.sum(residual * residual)
    curvature = jnp.sum(direction * product)
    step_size = norm_now / curvature
    solution_new = solution + step_size * direction
    residual_new = residual - step_size * product
    norm_next = jnp.sum(residual_new * residual_new)
    direction_new = residual_new + norm_next / norm_now * direction
    return (solution_new, residual_new, direction_new)
```

```python
import math

import jax
import jax.numpy as jnp
from jax import lax
from jax.experimental import pallas as pl
from jax.experimental.pallas import tpu as pltpu
from jax.sharding import Mesh, PartitionSpec as P

LANES = 128
PACK = 16
CHUNKS = 2
BF = jnp.bfloat16
F32 = jnp.float32


def trig_table(orders, length):
    points = jnp.arange(length, dtype=jnp.int32)
    phases = points[:, None] * orders[None, :] % length
    angles = phases.astype(jnp.float32) * (2.0 * math.pi / length)
    scaling_factor = 1.0 / math.sqrt(length / 2.0)
    stacked = jnp.stack([jnp.cos(angles), jnp.sin(angles)], axis=-1) * scaling_factor
    return stacked.reshape(length, 2 * orders.shape[0])


def plain_body(solution, residual, direction, noise_var, legendre, temporal, order_table):
    per_device, deg_dev, lat_all = legendre.shape
    latitude_rows_local, time_dev, longitude = direction.shape
    highest = lax.Precision.HIGHEST
    blk, tm = ("blk",), ("x", "core")
    lookup_table = trig_table(order_table, longitude)
    own_orders = lax.dynamic_slice_in_dim(order_table, lax.axis_index(blk) * per_device, per_device)
    own_degrees = lax.axis_index(tm) * deg_dev + jnp.arange(deg_dev, dtype=jnp.int32)
    keep_mask = own_degrees[None, :, None] >= own_orders[:, None, None]
    mask_applied = jnp.where(keep_mask, legendre, jnp.zeros_like(legendre))
    spectra = jnp.einsum("atj,jc->act", direction, lookup_table, precision=highest).astype(BF)
    cycles = lax.all_to_all(
        spectra.reshape(latitude_rows_local, -1), blk, split_axis=1, concat_axis=0, tiled=True
    )
    cycles = cycles.reshape(lat_all, per_device, 2, time_dev)
    full_table = lax.all_gather(mask_applied, tm, axis=1, tiled=True)
    coeffs = jnp.einsum("kla,akct->kclt", full_table, cycles, preferred_element_type=F32)
    coeffs = lax.all_to_all(coeffs, tm, split_axis=2, concat_axis=3, tiled=True)
    mixed = jnp.einsum("ltu,kclu->kclt", temporal, coeffs, precision=highest).astype(BF)
    returned = lax.all_to_all(mixed, tm, split_axis=3, concat_axis=2, tiled=True)
    terms = jnp.einsum("kla,kclt->takc", full_table, returned, preferred_element_type=F32)
    terms = terms.reshape(time_dev, lat_all, per_device * 2)
    column_entries = lax.all_to_all(terms, blk, split_axis=1, concat_axis=2, tiled=True)
    harmonic_synthesis = jnp.einsum("qpo,lo->pql", column_entries, lookup_table, precision=highest)
    product = harmonic_synthesis + noise_var * direction
    every = blk + tm
    norm_now = lax.psum(jnp.sum(residual * residual), every)
    curvature = lax.psum(jnp.sum(direction * product), every)
    step_size = norm_now / curvature
    solution_new = solution + step_size * direction
    residual_new = residual - step_size * product
    norm_next = lax.psum(jnp.sum(residual_new * residual_new), every)
    direction_new = residual_new + norm_next / norm_now * direction
    return (solution_new, residual_new, direction_new)


def swap_halves(v):
    half = LANES // 2
    return jnp.concatenate([v[..., half:], v[..., :half]], axis=-1)


def low_half(shape):
    return lax.broadcasted_iota(jnp.int32, shape, len(shape) - 1) < LANES // 2


def analysis_call(direction4, table):
    cycles, lo_n, hi_n, length = direction4.shape
    cols = table.shape[0]
    sub = 8
    steps = hi_n // sub

    parts_n = length // LANES

    def kernel(*refs):
        x_refs = refs[:parts_n]
        tab_ref, o_ref, s_ref = refs[parts_n:]
        h = pl.program_id(0)
        flat = [ref.reshape(cycles * lo_n * sub, LANES) for ref in x_refs]

        def pair(i, carry):
            parts = []
            for ii in range(2):
                for lo in range(lo_n):
                    at = pl.ds(lo * sub + 2 * i + ii, cycles, stride=lo_n * sub)
                    parts.append(jnp.concatenate([ref[at, :].astype(BF) for ref in flat], axis=1))
            x = jnp.concatenate(parts, axis=0)
            y = lax.dot_general(
                tab_ref[...], x, (((1,), (1,)), ((), ())), preferred_element_type=F32
            )
            for ii in range(2):
                s_ref[pl.ds(h * sub + 2 * i + ii, cols, stride=hi_n), :] = y[
                    :, ii * LANES : (ii + 1) * LANES
                ]
            return carry

        lax.fori_loop(0, sub // 2, pair, 0)

        @pl.when(h == steps - 1)
        def _():
            o_ref[...] = s_ref[...].reshape(cols, hi_n, LANES).astype(BF)

    return pl.pallas_call(
        kernel,
        out_shape=jax.ShapeDtypeStruct((cols, hi_n, LANES), BF),
        grid=(steps,),
        in_specs=[
            pl.BlockSpec((cycles, lo_n, sub, LANES), lambda h, p=p: (0, 0, h, p))
            for p in range(parts_n)
        ]
        + [pl.BlockSpec((cols, length), lambda h: (0, 0))],
        out_specs=pl.BlockSpec((cols, hi_n, LANES), lambda h: (0, 0, 0)),
        scratch_shapes=[pltpu.VMEM((cols * hi_n, LANES), F32)],
        compiler_params=pltpu.CompilerParams(vmem_limit_bytes=40 << 20),
        cost_estimate=pl.CostEstimate(
            flops=2 * cols * cycles * lo_n * hi_n * length,
            bytes_accessed=direction4.size * 4 + table.size * 2,
            transcendentals=0,
        ),
        name="analysis",
    )(*[direction4] * parts_n, table)


def degree_call(scalars, legendre, temporal, gathered, chunk, n_x, n_core):
    per_device, deg_dev, lat_all = legendre.shape
    time_all = temporal.shape[-1]
    n_pieces = len(gathered)
    nb, _, chunk_n, hi_n, _ = gathered[0].shape
    time_dev = 2 * hi_n
    kb = 4
    lb = 16
    n1 = chunk_n // kb
    n2 = deg_dev // lb
    pitch = deg_dev + 8
    rows = 2 * time_all
    first = chunk * n1

    def kernel(sc_ref, leg_ref, tmp_ref, *refs):
        r_refs = refs[:n_pieces]
        keep_ref, send_ref, c_ref, r_scr, g_scr = refs[n_pieces:]
        step = pl.program_id(0)
        low = low_half((hi_n, LANES))

        def masked(kk, k):
            order = sc_ref[1 + 2 * n_pieces + k]
            degree = sc_ref[0] + lax.broadcasted_iota(jnp.int32, (deg_dev, lat_all), 0)
            values = leg_ref[kk]
            return jnp.where(degree >= order, values, jnp.zeros_like(values))

        @pl.when(step < n1)
        def _():
            for kk in range(kb):
                for q in range(n_pieces):
                    base = sc_ref[1 + q] * time_dev
                    for c in range(2):
                        for p in range(nb // 2):
                            even = r_refs[q][2 * p, c, kk]
                            odd = r_refs[q][2 * p + 1, c, kk]
                            for lo in range(2):
                                at = pl.multiple_of(c * time_all + base + lo * hi_n, hi_n)
                                if lo == 0:
                                    v = jnp.where(low, even, swap_halves(odd))
                                else:
                                    v = jnp.where(low, swap_halves(even), odd)
                                r_scr[kk, pl.ds(at, hi_n), p * LANES : (p + 1) * LANES] = v
                k = step * kb + kk
                y = lax.dot_general(
                    masked(kk, k), r_scr[kk], (((1,), (1,)), ((), ())), preferred_element_type=F32
                )
                for c in range(2):
                    at = pl.multiple_of((k * 2 + c) * pitch, 8)
                    c_ref[pl.ds(at, deg_dev), :] = y[:, c * time_all : (c + 1) * time_all]

        @pl.when((step >= n1) & (step < n1 + n2))
        def _():
            for i in range(lb):
                at = (step - n1) * lb + i
                v = c_ref[pl.ds(at, 2 * chunk_n, stride=pitch), :].astype(BF)
                w = tmp_ref[i].astype(BF)
                c_ref[pl.ds(at, 2 * chunk_n, stride=pitch), :] = jnp.dot(
                    v, w, preferred_element_type=F32
                )

        @pl.when(step >= n1 + n2)
        def _():
            for kk in range(kb):
                k = (step - n1 - n2) * kb + kk
                m = masked(kk, k)
                for c in range(2):
                    at = pl.multiple_of((k * 2 + c) * pitch, 8)
                    v = c_ref[pl.ds(at, deg_dev), :].astype(BF)
                    g_scr[kk, c * time_all : (c + 1) * time_all, :] = lax.dot_general(
                        v, m, (((0,), (0,)), ((), ())), preferred_element_type=F32
                    ).astype(BF)
                for q in range(n_pieces):
                    base = sc_ref[1 + n_pieces + q] * time_dev
                    out = keep_ref if q < n_x else send_ref
                    for c in range(2):
                        for p in range(nb // 2):
                            at = pl.multiple_of(c * time_all + base, hi_n)
                            lanes = slice(p * LANES, (p + 1) * LANES)
                            v0 = g_scr[kk, pl.ds(at, hi_n), lanes]
                            v1 = g_scr[kk, pl.ds(at + hi_n, hi_n), lanes]
                            out[q % n_x, 2 * p, c, kk] = jnp.where(low, v0, swap_halves(v1))
                            out[q % n_x, 2 * p + 1, c, kk] = jnp.where(low, swap_halves(v0), v1)

    def leg_map(s, sc):
        return (
            first + jnp.where(s < n1, s, jnp.where(s < n1 + n2, n1 - 1, s - n1 - n2)),
            0,
            0,
        )

    piece = (nb, 2, chunk_n, hi_n, LANES)
    out_block = pl.BlockSpec(
        (n_x, nb, 2, kb, hi_n, LANES),
        lambda s, sc: (0, 0, 0, jnp.maximum(s - n1 - n2, 0), 0, 0),
    )
    out_shape = jax.ShapeDtypeStruct((n_x,) + piece, BF)
    flops = 4 * chunk_n * deg_dev * lat_all * rows + 2 * deg_dev * 2 * chunk_n * time_all**2
    return pl.pallas_call(
        kernel,
        out_shape=(out_shape, out_shape),
        grid_spec=pltpu.PrefetchScalarGridSpec(
            num_scalar_prefetch=1,
            grid=(n1 + n2 + n1,),
            in_specs=[
                pl.BlockSpec((kb, deg_dev, lat_all), leg_map),
                pl.BlockSpec(
                    (lb, time_all, time_all),
                    lambda s, sc: (jnp.clip(s - n1, 0, n2 - 1), 0, 0),
                ),
            ]
            + [
                pl.BlockSpec(
                    (nb, 2, kb, hi_n, LANES),
                    lambda s, sc: (0, 0, jnp.minimum(s, n1 - 1), 0, 0),
                )
            ]
            * n_pieces,
            out_specs=(out_block, out_block),
            scratch_shapes=[
                pltpu.VMEM((2 * chunk_n * pitch, time_all), F32),
                pltpu.VMEM((kb, rows, lat_all), BF),
                pltpu.VMEM((kb, rows, lat_all), BF),
            ],
        ),
        compiler_params=pltpu.CompilerParams(vmem_limit_bytes=40 << 20),
        cost_estimate=pl.CostEstimate(
            flops=flops,
            bytes_accessed=4 * chunk_n * deg_dev * lat_all
            + temporal.size * 4
            + 4 * n_pieces * gathered[0].size,
            transcendentals=0,
        ),
        name="degrees",
    )(scalars, legendre, temporal, *gathered)


def synthesis_call(received, table, previous, extra, scale):
    cols, hi_n, _ = received.shape
    length = table.shape[-1]
    lo_n = 2
    cycles = LANES // lo_n
    sub = 8
    jb = 512
    last = extra is not None
    n_in = 2 + (previous is not None) + (3 if last else 0)

    def kernel(*refs):
        rec_ref, tab_ref = refs[:2]
        at = 2
        prev_ref = None
        if previous is not None:
            prev_ref = refs[at]
            at += 1
        if last:
            noise_ref, dir_ref, res_ref = refs[at : at + 3]
            at += 3
        o_ref = refs[at]
        at += 1
        if last:
            sum_ref = refs[at]
            at += 1
        s_ref, p_ref = refs[at : at + 2]
        h, j = pl.program_id(0), pl.program_id(1)

        @pl.when((h == 0) & (j == 0))
        def _():
            s_ref[...] = rec_ref[...].astype(F32).reshape(cols * hi_n, LANES)
            if last:
                sum_ref[...] = jnp.zeros_like(sum_ref)

        def one(i, carry):
            v = s_ref[pl.ds(h * sub + i, cols, stride=hi_n), :].astype(BF)
            y = lax.dot_general(
                v, tab_ref[...], (((0,), (0,)), ((), ())), preferred_element_type=F32
            )
            y = y * scale
            for lo in range(lo_n):
                for part in range(jb // LANES):
                    p_ref[part, pl.ds(lo * sub + i, cycles, stride=lo_n * sub), :] = y[
                        lo * cycles : (lo + 1) * cycles, part * LANES : (part + 1) * LANES
                    ]
            return carry

        lax.fori_loop(0, sub, one, 0)
        group = 8

        def finish(i, carry):
            carry = list(carry)
            block = pl.ds(i * group, group)
            for part in range(jb // LANES):
                lanes = slice(part * LANES, (part + 1) * LANES)
                span = group * lo_n * sub
                rows = pl.ds(pl.multiple_of(i * span, span), span)
                p = p_ref[part, rows, :].reshape(group, lo_n, sub, LANES)
                if prev_ref is not None:
                    p = p + prev_ref[block, :, :, lanes]
                if last:
                    d = dir_ref[block, :, :, lanes]
                    r = res_ref[block, :, :, lanes]
                    p = p + noise_ref[block, :, :, lanes] * d
                    for n, term in enumerate((r * r, d * p, r * p, p * p)):
                        carry[n] = carry[n] + jnp.sum(term, axis=(0, 1))
                o_ref[block, :, :, lanes] = p
            return tuple(carry)

        zero = (jnp.zeros((sub, LANES), F32),) * 4
        sums = lax.fori_loop(0, cycles // group, finish, zero)
        if last:
            for n in range(4):
                sum_ref[n] = sum_ref[n] + sums[n]

    grid_block = pl.BlockSpec((cycles, lo_n, sub, jb), lambda h, j: (0, 0, h, j))
    in_specs = [
        pl.BlockSpec((cols, hi_n, LANES), lambda h, j: (0, 0, 0)),
        pl.BlockSpec((cols, jb), lambda h, j: (0, j)),
    ] + [grid_block] * (n_in - 2)
    shape4 = (cycles, lo_n, hi_n, length)
    out_shape = [jax.ShapeDtypeStruct(shape4, F32)]
    out_specs = [grid_block]
    if last:
        out_shape.append(jax.ShapeDtypeStruct((4, sub, LANES), F32))
        out_specs.append(pl.BlockSpec((4, sub, LANES), lambda h, j: (0, 0, 0)))
    args = [received, table]
    if previous is not None:
        args.append(previous)
    if last:
        args += list(extra)
    return pl.pallas_call(
        kernel,
        out_shape=tuple(out_shape),
        grid=(hi_n // sub, length // jb),
        in_specs=in_specs,
        out_specs=tuple(out_specs),
        scratch_shapes=[
            pltpu.VMEM((cols * hi_n, LANES), F32),
            pltpu.VMEM((jb // LANES, cycles * lo_n * sub, LANES), F32),
        ],
        compiler_params=pltpu.CompilerParams(vmem_limit_bytes=48 << 20),
        cost_estimate=pl.CostEstimate(
            flops=2 * cols * LANES * hi_n * length,
            bytes_accessed=4 * cycles * lo_n * hi_n * length * (n_in - 1),
            transcendentals=0,
        ),
        name="synthesis",
    )(*args)


def sum_everywhere(values, mesh):
    for name in ("core", "x", "blk"):
        n = mesh.shape[name]
        if n & (n - 1):
            total = values
            for s in range(1, n):
                total = total + lax.ppermute(values, name, [(i, (i + s) % n) for i in range(n)])
            values = total
            continue
        step = 1
        while step < n:
            values = values + lax.ppermute(values, name, [(i, i ^ step) for i in range(n)])
            step *= 2
    return values


def fast_body(mesh, solution, residual, direction, noise_var, legendre, temporal, order_table):
    per_device, deg_dev, lat_all = legendre.shape
    cycles, time_dev, longitude = direction.shape
    nb, n_x, n_core = (mesh.shape[name] for name in ("blk", "x", "core"))
    lo_n = LANES // cycles
    hi_n = time_dev // lo_n
    chunk_n = per_device // CHUNKS
    cols = nb * 2 * chunk_n
    blk_i, x_i, core_i = (lax.axis_index(name) for name in ("blk", "x", "core"))
    grouped = order_table.reshape(nb, per_device)
    own_orders = lax.dynamic_slice_in_dim(order_table, blk_i * per_device, per_device)
    shape4 = (cycles, lo_n, hi_n, longitude)
    direction4, noise4, residual4 = (v.reshape(shape4) for v in (direction, noise_var, residual))
    quarter = (longitude // 4) * 3

    def table_of(chunk):
        orders = grouped[:, chunk * chunk_n : (chunk + 1) * chunk_n]
        points = jnp.arange(longitude, dtype=jnp.int32)
        turn = jnp.arange(2, dtype=jnp.int32) * quarter
        phases = orders[:, None, :, None] * points + turn[None, :, None, None]
        angles = (phases % longitude).astype(F32) * (2.0 * math.pi / longitude)
        return jnp.cos(angles).astype(BF).reshape(cols, longitude)

    forth = [jnp.mod(x_i - s, n_x) * n_core + (core_i + o) % n_core for o in range(2) for s in range(n_x)]
    back = [jnp.mod(x_i + s, n_x) * n_core + (core_i + o) % n_core for o in range(2) for s in range(n_x)]
    base = (x_i * n_core + core_i) * deg_dev
    header = jnp.stack([base] + forth + back).astype(jnp.int32)
    swap = [(i, (i + 1) % n_core) for i in range(n_core)]

    def shift(v, s):
        return lax.ppermute(v, "x", [(i, (i + s) % n_x) for i in range(n_x)])

    tables, pieces = [], []
    for g in range(CHUNKS):
        with jax.named_scope(f"forth{g}"):
            table = table_of(g)
            tables.append(table)
            spectra = analysis_call(direction4, table)
            mine = lax.all_to_all(
                spectra.reshape(nb, 2, chunk_n, hi_n, LANES),
                "blk",
                split_axis=0,
                concat_axis=0,
                tiled=True,
            )
            own = [mine] + [shift(mine, s) for s in range(1, n_x)]
            pieces.append(own + [lax.ppermute(v, "core", swap) for v in own])
    received = []
    for g in range(CHUNKS):
        with jax.named_scope(f"degrees{g}"):
            scalars = jnp.concatenate([header, own_orders[g * chunk_n : (g + 1) * chunk_n]])
            keep, send = degree_call(scalars, legendre, temporal, pieces[g], g, n_x, n_core)
        with jax.named_scope(f"back{g}"):
            other = lax.ppermute(send, "core", swap)
            halves = [keep[s].astype(F32) + other[s].astype(F32) for s in range(n_x)]
            total = halves[0]
            for s in range(1, n_x):
                total = total + shift(halves[s].astype(BF), s).astype(F32)
            received.append(
                lax.all_to_all(total.astype(BF), "blk", split_axis=0, concat_axis=0, tiled=True)
            )
    product = None
    scale = 2.0 / longitude
    for g in range(CHUNKS):
        with jax.named_scope(f"synthesis{g}"):
            extra = (noise4, direction4, residual4) if g == CHUNKS - 1 else None
            out = synthesis_call(
                received[g].reshape(cols, hi_n, LANES), tables[g], product, extra, scale
            )
            product = out[0]
    sums = out[1]
    with jax.named_scope("sums"):
        sums = sum_everywhere(jnp.sum(sums, axis=1), mesh)
        norm_now, curvature, cross, square = (v for v in jnp.sum(sums, axis=1))
    product = product.reshape(direction.shape)
    step_size = norm_now / curvature
    norm_next = norm_now - 2.0 * (step_size * cross) + step_size * (step_size * square)
    solution_new = solution + step_size * direction
    residual_new = residual - step_size * product
    direction_new = residual_new + norm_next / norm_now * direction
    return (solution_new, residual_new, direction_new)


def solution(mesh):
    n_core = 2 if mesh.shape["tm"] % 2 == 0 else 1
    n_x = mesh.shape["tm"] // n_core
    nb = mesh.shape["blk"]
    inner = Mesh(mesh.devices.reshape(nb, n_x, n_core), ("blk", "x", "core"))
    tm = ("x", "core")

    def body(*args):
        direction, legendre = args[2], args[4]
        cycles, time_dev, longitude = direction.shape
        fits = (
            n_core == 2
            and 2 * cycles == LANES
            and time_dev == 2 * PACK
            and nb % 2 == 0
            and longitude % 512 == 0
            and legendre.shape[0] % (4 * CHUNKS) == 0
            and legendre.shape[1] % PACK == 0
            and legendre.shape[2] % LANES == 0
            and args[5].shape[-1] % LANES == 0
        )
        if fits:
            return fast_body(inner, *args)
        return plain_body(*args)

    grid = P("blk", tm, None)
    return jax.shard_map(
        body,
        mesh=inner,
        in_specs=(grid, grid, grid, grid, grid, P(tm, None, None), P()),
        out_specs=(grid, grid, grid),
        check_vma=False,
    )
```

```python
import math

import jax
import jax.numpy as jnp
from jax import lax
from jax.experimental import pallas as pl
from jax.experimental.pallas import tpu as pltpu
from jax.sharding import Mesh, PartitionSpec as P


LANES = 128
PACK = 16
CHUNKS = 4
BF = jnp.bfloat16
F32 = jnp.float32


def trig_table(orders, length):
    points = jnp.arange(length, dtype=jnp.int32)
    phases = points[:, None] * orders[None, :] % length
    angles = phases.astype(jnp.float32) * (2.0 * math.pi / length)
    scaling_factor = 1.0 / math.sqrt(length / 2.0)
    stacked = jnp.stack([jnp.cos(angles), jnp.sin(angles)], axis=-1) * scaling_factor
    return stacked.reshape(length, 2 * orders.shape[0])


def plain_body(solution, residual, direction, noise_var, legendre, temporal, order_table):
    per_device, deg_dev, lat_all = legendre.shape
    latitude_rows_local, time_dev, longitude = direction.shape
    highest = lax.Precision.HIGHEST
    blk, tm = ("blk",), ("x", "core")
    lookup_table = trig_table(order_table, longitude)
    own_orders = lax.dynamic_slice_in_dim(order_table, lax.axis_index(blk) * per_device, per_device)
    own_degrees = lax.axis_index(tm) * deg_dev + jnp.arange(deg_dev, dtype=jnp.int32)
    keep_mask = own_degrees[None, :, None] >= own_orders[:, None, None]
    mask_applied = jnp.where(keep_mask, legendre, jnp.zeros_like(legendre))
    spectra = jnp.einsum("atj,jc->act", direction, lookup_table, precision=highest).astype(BF)
    cycles = lax.all_to_all(
        spectra.reshape(latitude_rows_local, -1), blk, split_axis=1, concat_axis=0, tiled=True
    )
    cycles = cycles.reshape(lat_all, per_device, 2, time_dev)
    full_table = lax.all_gather(mask_applied, tm, axis=1, tiled=True)
    coeffs = jnp.einsum("kla,akct->kclt", full_table, cycles, preferred_element_type=F32)
    coeffs = lax.all_to_all(coeffs, tm, split_axis=2, concat_axis=3, tiled=True)
    mixed = jnp.einsum("ltu,kclu->kclt", temporal, coeffs, precision=highest).astype(BF)
    returned = lax.all_to_all(mixed, tm, split_axis=3, concat_axis=2, tiled=True)
    terms = jnp.einsum("kla,kclt->takc", full_table, returned, preferred_element_type=F32)
    terms = terms.reshape(time_dev, lat_all, per_device * 2)
    column_entries = lax.all_to_all(terms, blk, split_axis=1, concat_axis=2, tiled=True)
    harmonic_synthesis = jnp.einsum("qpo,lo->pql", column_entries, lookup_table, precision=highest)
    product = harmonic_synthesis + noise_var * direction
    every = blk + tm
    norm_now = lax.psum(jnp.sum(residual * residual), every)
    curvature = lax.psum(jnp.sum(direction * product), every)
    step_size = norm_now / curvature
    solution_new = solution + step_size * direction
    residual_new = residual - step_size * product
    norm_next = lax.psum(jnp.sum(residual_new * residual_new), every)
    direction_new = residual_new + norm_next / norm_now * direction
    return (solution_new, residual_new, direction_new)


def swap_halves(v):
    half = LANES // 2
    return jnp.concatenate([v[..., half:], v[..., :half]], axis=-1)


def low_half(shape):
    return lax.broadcasted_iota(jnp.int32, shape, len(shape) - 1) < LANES // 2


def analysis_call(direction4, tables):
    cycles, lo_n, hi_n, length = direction4.shape
    cols = tables[0].shape[0]
    n_tab = len(tables)
    sub = 8
    steps = hi_n // sub
    parts_n = length // LANES

    def kernel(*refs):
        x_refs = refs[:parts_n]
        tab_refs = refs[parts_n : parts_n + n_tab]
        o_refs = refs[parts_n + n_tab : parts_n + 2 * n_tab]
        s_ref = refs[-1]
        h = pl.program_id(0)
        flat = [ref.reshape(cycles * lo_n * sub, LANES) for ref in x_refs]

        def pair(i, carry):
            parts = []
            for ii in range(2):
                for lo in range(lo_n):
                    at = pl.ds(lo * sub + 2 * i + ii, cycles, stride=lo_n * sub)
                    parts.append(jnp.concatenate([ref[at, :].astype(BF) for ref in flat], axis=1))
            x = jnp.concatenate(parts, axis=0)
            for n in range(n_tab):
                y = lax.dot_general(
                    tab_refs[n][...], x, (((1,), (1,)), ((), ())), preferred_element_type=F32
                )
                for ii in range(2):
                    s_ref[n, pl.ds(h * sub + 2 * i + ii, cols, stride=hi_n), :] = y[
                        :, ii * LANES : (ii + 1) * LANES
                    ]
            return carry

        lax.fori_loop(0, sub // 2, pair, 0)

        @pl.when(h == steps - 1)
        def _():
            for n in range(n_tab):
                o_refs[n][...] = s_ref[n].reshape(cols, hi_n, LANES).astype(BF)

    out = jax.ShapeDtypeStruct((cols, hi_n, LANES), BF)
    return pl.pallas_call(
        kernel,
        out_shape=(out,) * n_tab,
        grid=(steps,),
        in_specs=[
            pl.BlockSpec((cycles, lo_n, sub, LANES), lambda h, p=p: (0, 0, h, p))
            for p in range(parts_n)
        ]
        + [pl.BlockSpec((cols, length), lambda h: (0, 0))] * n_tab,
        out_specs=(pl.BlockSpec((cols, hi_n, LANES), lambda h: (0, 0, 0)),) * n_tab,
        scratch_shapes=[pltpu.VMEM((n_tab, cols * hi_n, LANES), F32)],
        compiler_params=pltpu.CompilerParams(vmem_limit_bytes=60 << 20),
        cost_estimate=pl.CostEstimate(
            flops=2 * n_tab * cols * cycles * lo_n * hi_n * length,
            bytes_accessed=direction4.size * 4 + n_tab * cols * length * 2,
            transcendentals=0,
        ),
        name="analysis",
    )(*[direction4] * parts_n, *tables)


def degree_call(scalars, legendre, temporal, gathered, chunk, n_x):
    _, deg_dev, lat_all = legendre.shape
    time_all = temporal.shape[-1]
    n_pieces = len(gathered)
    nb, _, chunk_n, hi_n, _ = gathered[0].shape
    time_dev = 2 * hi_n
    kb = 4
    lb = 16
    n1 = chunk_n // kb
    n2 = deg_dev // lb
    pitch = deg_dev + 8
    rows = 2 * time_all
    first = chunk * n1

    def kernel(sc_ref, leg_ref, tmp_ref, *refs):
        r_refs = refs[:n_pieces]
        keep_ref, send_ref, c_ref, r_scr, g_scr = refs[n_pieces:]
        step = pl.program_id(0)
        low = low_half((hi_n, LANES))

        def masked(kk, k):
            order = sc_ref[1 + 2 * n_pieces + k]
            degree = sc_ref[0] + lax.broadcasted_iota(jnp.int32, (deg_dev, lat_all), 0)
            values = leg_ref[kk]
            return jnp.where(degree >= order, values, jnp.zeros_like(values))

        @pl.when(step < n1)
        def _():
            for kk in range(kb):
                for q in range(n_pieces):
                    base = sc_ref[1 + q] * time_dev
                    for c in range(2):
                        for p in range(nb // 2):
                            even = r_refs[q][2 * p, c, kk]
                            odd = r_refs[q][2 * p + 1, c, kk]
                            for lo in range(2):
                                at = pl.multiple_of(c * time_all + base + lo * hi_n, hi_n)
                                if lo == 0:
                                    v = jnp.where(low, even, swap_halves(odd))
                                else:
                                    v = jnp.where(low, swap_halves(even), odd)
                                r_scr[kk, pl.ds(at, hi_n), p * LANES : (p + 1) * LANES] = v
                k = step * kb + kk
                y = lax.dot_general(
                    masked(kk, k), r_scr[kk], (((1,), (1,)), ((), ())), preferred_element_type=F32
                )
                for c in range(2):
                    at = pl.multiple_of((k * 2 + c) * pitch, 8)
                    c_ref[pl.ds(at, deg_dev), :] = y[:, c * time_all : (c + 1) * time_all]

        @pl.when((step >= n1) & (step < n1 + n2))
        def _():
            for i in range(lb):
                at = (step - n1) * lb + i
                v = c_ref[pl.ds(at, 2 * chunk_n, stride=pitch), :].astype(BF)
                w = tmp_ref[i]
                c_ref[pl.ds(at, 2 * chunk_n, stride=pitch), :] = jnp.dot(
                    v, w, preferred_element_type=F32
                )

        @pl.when(step >= n1 + n2)
        def _():
            for kk in range(kb):
                k = (step - n1 - n2) * kb + kk
                m = masked(kk, k)
                for c in range(2):
                    at = pl.multiple_of((k * 2 + c) * pitch, 8)
                    v = c_ref[pl.ds(at, deg_dev), :].astype(BF)
                    g_scr[kk, c * time_all : (c + 1) * time_all, :] = lax.dot_general(
                        v, m, (((0,), (0,)), ((), ())), preferred_element_type=F32
                    ).astype(BF)
                for q in range(n_pieces):
                    base = sc_ref[1 + n_pieces + q] * time_dev
                    out = keep_ref if q < n_x else send_ref
                    for c in range(2):
                        for p in range(nb // 2):
                            at = pl.multiple_of(c * time_all + base, hi_n)
                            lanes = slice(p * LANES, (p + 1) * LANES)
                            v0 = g_scr[kk, pl.ds(at, hi_n), lanes]
                            v1 = g_scr[kk, pl.ds(at + hi_n, hi_n), lanes]
                            out[q % n_x, 2 * p, c, kk] = jnp.where(low, v0, swap_halves(v1))
                            out[q % n_x, 2 * p + 1, c, kk] = jnp.where(low, swap_halves(v0), v1)

    def leg_map(s, sc):
        return (
            first + jnp.where(s < n1, s, jnp.where(s < n1 + n2, n1 - 1, s - n1 - n2)),
            0,
            0,
        )

    piece = (nb, 2, chunk_n, hi_n, LANES)
    out_block = pl.BlockSpec(
        (n_x, nb, 2, kb, hi_n, LANES),
        lambda s, sc: (0, 0, 0, jnp.maximum(s - n1 - n2, 0), 0, 0),
    )
    out_shape = jax.ShapeDtypeStruct((n_x,) + piece, BF)
    flops = 4 * chunk_n * deg_dev * lat_all * rows + 2 * deg_dev * 2 * chunk_n * time_all**2
    return pl.pallas_call(
        kernel,
        out_shape=(out_shape, out_shape),
        grid_spec=pltpu.PrefetchScalarGridSpec(
            num_scalar_prefetch=1,
            grid=(n1 + n2 + n1,),
            in_specs=[
                pl.BlockSpec((kb, deg_dev, lat_all), leg_map),
                pl.BlockSpec(
                    (lb, time_all, time_all),
                    lambda s, sc: (jnp.clip(s - n1, 0, n2 - 1), 0, 0),
                ),
            ]
            + [
                pl.BlockSpec(
                    (nb, 2, kb, hi_n, LANES),
                    lambda s, sc: (0, 0, jnp.minimum(s, n1 - 1), 0, 0),
                )
            ]
            * n_pieces,
            out_specs=(out_block, out_block),
            scratch_shapes=[
                pltpu.VMEM((2 * chunk_n * pitch, time_all), F32),
                pltpu.VMEM((kb, rows, lat_all), BF),
                pltpu.VMEM((kb, rows, lat_all), BF),
            ],
        ),
        compiler_params=pltpu.CompilerParams(vmem_limit_bytes=60 << 20),
        cost_estimate=pl.CostEstimate(
            flops=flops,
            bytes_accessed=4 * chunk_n * deg_dev * lat_all
            + temporal.size * 2
            + 4 * n_pieces * gathered[0].size,
            transcendentals=0,
        ),
        name="degrees",
    )(scalars, legendre, temporal, *gathered)


def synthesis_call(received, tables, previous, fields, scale):
    n_tab = len(received)
    cols, hi_n, _ = received[0].shape
    length = tables[0].shape[-1]
    lo_n = 2
    cycles = LANES // lo_n
    sub = 8
    jb = 512
    last = previous is not None
    n_grid = 3 if last else 2

    def kernel(*refs):
        rec_refs = refs[:n_tab]
        tab_refs = refs[n_tab : 2 * n_tab]
        grid_refs = refs[2 * n_tab : 2 * n_tab + n_grid]
        o_ref = refs[2 * n_tab + n_grid]
        sum_ref = refs[2 * n_tab + n_grid + 1] if last else None
        s_ref = refs[-1]
        h, j = pl.program_id(0), pl.program_id(1)
        if last:
            p_ref = o_ref.at[h, j]
            d_ref, r_ref = (refs[2 * n_tab + n_grid + n].at[h, j] for n in (2, 3))
        else:
            p_ref = refs[-2]

        @pl.when((h == 0) & (j == 0))
        def _():
            for n in range(n_tab):
                s_ref[n * cols * hi_n : (n + 1) * cols * hi_n, :] = (
                    rec_refs[n][...].astype(F32).reshape(cols * hi_n, LANES)
                )
            if last:
                sum_ref[...] = jnp.zeros_like(sum_ref)

        def one(i, carry):
            y = None
            for n in range(n_tab):
                at = pl.ds(n * cols * hi_n + h * sub + i, cols, stride=hi_n)
                v = s_ref[at, :].astype(BF)
                term = lax.dot_general(
                    v, tab_refs[n][...], (((0,), (0,)), ((), ())), preferred_element_type=F32
                )
                y = term if y is None else y + term
            y = y * scale
            for lo in range(lo_n):
                for part in range(jb // LANES):
                    p_ref[part, pl.ds(lo * sub + i, cycles, stride=lo_n * sub), :] = y[
                        lo * cycles : (lo + 1) * cycles, part * LANES : (part + 1) * LANES
                    ]
            return carry

        lax.fori_loop(0, sub, one, 0)
        group = 8

        def finish(i, carry):
            carry = list(carry)
            block = pl.ds(i * group, group)
            for part in range(jb // LANES):
                lanes = slice(part * LANES, (part + 1) * LANES)
                span = group * lo_n * sub
                rows = pl.ds(pl.multiple_of(i * span, span), span)
                p = p_ref[part, rows, :].reshape(group, lo_n, sub, LANES)
                if last:
                    p = p + grid_refs[0][block, :, :, lanes]
                    d = grid_refs[1][block, :, :, lanes]
                    r = grid_refs[2][block, :, :, lanes]
                    for n, term in enumerate((r * r, d * p, r * p, p * p)):
                        carry[n] = carry[n] + jnp.sum(term, axis=(0, 1))
                    for ref, v in ((p_ref, p), (d_ref, d), (r_ref, r)):
                        ref[part, rows, :] = v.reshape(span, LANES)
                else:
                    p = p + grid_refs[0][block, :, :, lanes] * grid_refs[1][block, :, :, lanes]
                    o_ref[block, :, :, lanes] = p
            return tuple(carry)

        zero = (jnp.zeros((sub, LANES), F32),) * 4
        sums = lax.fori_loop(0, cycles // group, finish, zero)
        if last:
            for n in range(4):
                sum_ref[n : n + 1, :] = sum_ref[n : n + 1, :] + jnp.sum(
                    sums[n], axis=0, keepdims=True
                )

    grid_block = pl.BlockSpec((cycles, lo_n, sub, jb), lambda h, j: (0, 0, h, j))
    in_specs = (
        [pl.BlockSpec((cols, hi_n, LANES), lambda h, j: (0, 0, 0))] * n_tab
        + [pl.BlockSpec((cols, jb), lambda h, j: (0, j))] * n_tab
        + [grid_block] * n_grid
    )
    tile_rows = cycles * lo_n * sub
    if last:
        held = pltpu.VMEM((hi_n // sub, length // jb, jb // LANES, tile_rows, LANES), F32)
        whole = pl.BlockSpec(memory_space=pltpu.VMEM)
        out_shape = [held, jax.ShapeDtypeStruct((sub, LANES), F32), held, held]
        out_specs = [whole, pl.BlockSpec((sub, LANES), lambda h, j: (0, 0)), whole, whole]
    else:
        out_shape = [jax.ShapeDtypeStruct((cycles, lo_n, hi_n, length), F32)]
        out_specs = [grid_block]
    grids = ((previous,) if last else ()) + tuple(fields)
    return pl.pallas_call(
        kernel,
        out_shape=tuple(out_shape),
        grid=(hi_n // sub, length // jb),
        in_specs=in_specs,
        out_specs=tuple(out_specs),
        scratch_shapes=([] if last else [pltpu.VMEM((jb // LANES, tile_rows, LANES), F32)])
        + [pltpu.VMEM((n_tab * cols * hi_n, LANES), F32)],
        compiler_params=pltpu.CompilerParams(vmem_limit_bytes=(24 << 20) if last else (60 << 20)),
        cost_estimate=pl.CostEstimate(
            flops=2 * n_tab * cols * LANES * hi_n * length,
            bytes_accessed=4 * cycles * lo_n * hi_n * length * (n_grid + 1),
            transcendentals=0,
        ),
        name="synthesis",
    )(*received, *tables, *grids)


def update_call(sums, solution4, held):
    cycles, lo_n, hi_n, length = solution4.shape
    _, steps_j, parts, _, _ = held[0].shape
    sub, jb = hi_n // held[0].shape[0], length // steps_j
    group = 8
    span = group * lo_n * sub

    n_sums = len(sums)

    def kernel(*refs):
        x_ref, p_ref, r_ref, d_ref, xo_ref, ro_ref, do_ref = refs[n_sums:]
        h, j = pl.program_id(0), pl.program_id(1)
        total = refs[0][...]
        for ref in refs[1:n_sums]:
            total = total + ref[...]
        norm_now, curvature, cross, square = (
            jnp.sum(total[n : n + 1], keepdims=True) for n in range(4)
        )
        step = norm_now / curvature
        norm_next = norm_now - 2.0 * (step * cross) + step * (step * square)
        ratio = norm_next / norm_now

        def some(i, carry):
            block = pl.ds(i * group, group)
            rows = pl.ds(pl.multiple_of(i * span, span), span)
            for part in range(parts):
                lanes = slice(part * LANES, (part + 1) * LANES)
                p, r, d = (
                    ref[h, j, part, rows, :].reshape(group, lo_n, sub, LANES)
                    for ref in (p_ref, r_ref, d_ref)
                )
                xo_ref[block, :, :, lanes] = x_ref[block, :, :, lanes] + step * d
                r = r - step * p
                ro_ref[block, :, :, lanes] = r
                do_ref[block, :, :, lanes] = r + ratio * d
            return carry

        lax.fori_loop(0, cycles // group, some, 0)

    spec = pl.BlockSpec((cycles, lo_n, sub, jb), lambda h, j: (0, 0, h, j))
    size = solution4.size
    return pl.pallas_call(
        kernel,
        out_shape=(jax.ShapeDtypeStruct(solution4.shape, F32),) * 3,
        grid=(hi_n // sub, steps_j),
        in_specs=[pl.BlockSpec(sums[0].shape, lambda h, j: (0, 0))] * n_sums
        + [spec]
        + [pl.BlockSpec(memory_space=pltpu.VMEM)] * 3,
        out_specs=(spec,) * 3,
        compiler_params=pltpu.CompilerParams(vmem_limit_bytes=24 << 20),
        cost_estimate=pl.CostEstimate(
            flops=6 * size, bytes_accessed=16 * size, transcendentals=0
        ),
        name="update",
    )(*sums, solution4, *(pltpu.with_memory_space_constraint(v, pltpu.VMEM) for v in held))


def add_call(values):
    def kernel(*refs):
        total = refs[0][...]
        for ref in refs[1:-1]:
            total = total + ref[...]
        refs[-1][...] = total

    return pl.pallas_call(
        kernel,
        out_shape=jax.ShapeDtypeStruct(values[0].shape, F32),
        compiler_params=pltpu.CompilerParams(vmem_limit_bytes=1 << 20),
        name="add",
    )(*values)


def sum_parts(values, n_blk, n_x, n_core):
    def stage(v, axes, perms):
        return [v] + [lax.ppermute(v, axes, perm) for perm in perms]

    n_tm = n_x * n_core
    tm = [[(i, (i + s) % n_tm) for i in range(n_tm)] for s in range(1, n_tm)]
    pair = [[(i, i ^ 1) for i in range(n_blk)]]
    rest = [[(i, (i + s) % n_blk) for i in range(n_blk)] for s in range(2, n_blk, 2)]
    values = add_call(stage(values, ("x", "core"), tm))
    values = add_call(stage(values, "blk", pair))
    return stage(values, "blk", rest)


def sine_table(phases, length):
    folded = jnp.abs(phases - length // 2) - length // 4
    x = folded.astype(F32) * (2.0 * math.pi / length)
    z = x * x
    value = jnp.full_like(z, -1.0 / math.factorial(11))
    for n in (9, 7, 5, 3, 1):
        value = value * z + (1.0 if n % 4 == 1 else -1.0) / math.factorial(n)
    return value * x


def fast_body(mesh, solution, residual, direction, noise_var, legendre, temporal, order_table):
    per_device, deg_dev, _ = legendre.shape
    cycles, time_dev, longitude = direction.shape
    nb, n_x, n_core = (mesh.shape[name] for name in ("blk", "x", "core"))
    lo_n = LANES // cycles
    hi_n = time_dev // lo_n
    chunk_n = per_device // CHUNKS
    cols = nb * 2 * chunk_n
    blk_i, x_i, core_i = (lax.axis_index(name) for name in ("blk", "x", "core"))
    grouped = order_table.reshape(nb, per_device)
    own_orders = lax.dynamic_slice_in_dim(order_table, blk_i * per_device, per_device)
    shape4 = (cycles, lo_n, hi_n, longitude)
    direction4, noise4, residual4 = (v.reshape(shape4) for v in (direction, noise_var, residual))
    quarter = (longitude // 4) * 3

    def table_of(chunk):
        orders = grouped[:, chunk * chunk_n : (chunk + 1) * chunk_n]
        points = jnp.arange(longitude, dtype=jnp.int32)
        turn = jnp.arange(2, dtype=jnp.int32) * quarter
        phases = orders[:, None, :, None] * points + turn[None, :, None, None]
        return sine_table(phases % longitude, longitude).astype(BF).reshape(cols, longitude)

    forth = [jnp.mod(x_i - s, n_x) * n_core + (core_i + o) % n_core for o in range(2) for s in range(n_x)]
    back = [jnp.mod(x_i + s, n_x) * n_core + (core_i + o) % n_core for o in range(2) for s in range(n_x)]
    base = (x_i * n_core + core_i) * deg_dev
    header = jnp.stack([base] + forth + back).astype(jnp.int32)
    swap = [(i, (i + 1) % n_core) for i in range(n_core)]

    def shift(v, s):
        return lax.ppermute(v, "x", [(i, (i + s) % n_x) for i in range(n_x)])

    def across(v):
        return lax.all_to_all(v, "blk", split_axis=0, concat_axis=0, tiled=True)

    tables = [table_of(0)]
    spectra = list(analysis_call(direction4, tables))
    piece = (nb, 2, chunk_n, hi_n, LANES)
    tables += [table_of(g) for g in range(1, CHUNKS)]
    spectra += list(analysis_call(direction4, tables[1:]))
    temporal_narrow = temporal.astype(BF)
    received = []
    for g in range(CHUNKS):
        mine = across(spectra[g].reshape(piece))
        own = [mine] + [shift(mine, s) for s in range(1, n_x)]
        pieces = own + [lax.ppermute(v, "core", swap) for v in own]
        scalars = jnp.concatenate([header, own_orders[g * chunk_n : (g + 1) * chunk_n]])
        keep, send = degree_call(scalars, legendre, temporal_narrow, pieces, g, n_x)
        other = lax.ppermute(send, "core", swap)
        halves = [keep[s].astype(F32) + other[s].astype(F32) for s in range(n_x)]
        halves = [halves[0].astype(BF)] + [v.astype(BF) for v in halves[1:]]
        parts = [shift(halves[s], s) for s in range(1, n_x)]
        total = halves[0].astype(F32)
        for part in parts:
            total = total + part.astype(F32)
        total = total.astype(BF)
        received.append(across(total).reshape(cols, hi_n, LANES))
    scale = 2.0 / longitude
    (partial,) = synthesis_call(received[:-1], tables[:-1], None, (noise4, direction4), scale)
    product, sums, near_d, near_r = synthesis_call(
        received[-1:], tables[-1:], partial, (direction4, residual4), scale
    )
    sums = sum_parts(sums, nb, n_x, n_core)
    out = update_call(sums, solution.reshape(shape4), (product, near_r, near_d))
    return tuple(v.reshape(direction.shape) for v in out)


def solution(mesh):
    n_core = 2 if mesh.shape["tm"] % 2 == 0 else 1
    n_x = mesh.shape["tm"] // n_core
    nb = mesh.shape["blk"]
    inner = Mesh(mesh.devices.reshape(nb, n_x, n_core), ("blk", "x", "core"))
    tm = ("x", "core")

    def body(*args):
        direction, legendre = args[2], args[4]
        cycles, time_dev, longitude = direction.shape
        fits = (
            n_core == 2
            and 2 * cycles == LANES
            and time_dev == 2 * PACK
            and nb % 2 == 0
            and longitude % 512 == 0
            and legendre.shape[0] % (4 * CHUNKS) == 0
            and legendre.shape[1] % PACK == 0
            and legendre.shape[2] % LANES == 0
            and args[5].shape[-1] % LANES == 0
        )
        if fits:
            return fast_body(inner, *args)
        return plain_body(*args)

    grid = P("blk", tm, None)
    return jax.shard_map(
        body,
        mesh=inner,
        in_specs=(grid, grid, grid, grid, grid, P(tm, None, None), P()),
        out_specs=(grid, grid, grid),
        check_vma=False,
    )
```

```python
import math

import jax
import jax.numpy as jnp
from jax import lax
from jax.experimental import pallas as pl
from jax.experimental.pallas import tpu as pltpu
from jax.sharding import Mesh, PartitionSpec as P


LANES = 128
PACK = 16
PLAN = ((0, 0), (1, 0), (1, 1), (0, 1))
CHUNKS = len(PLAN)
BF = jnp.bfloat16
F32 = jnp.float32


def trig_table(orders, length):
    points = jnp.arange(length, dtype=jnp.int32)
    phases = points[:, None] * orders[None, :] % length
    angles = phases.astype(jnp.float32) * (2.0 * math.pi / length)
    scaling_factor = 1.0 / math.sqrt(length / 2.0)
    stacked = jnp.stack([jnp.cos(angles), jnp.sin(angles)], axis=-1) * scaling_factor
    return stacked.reshape(length, 2 * orders.shape[0])


def plain_body(solution, residual, direction, noise_var, legendre, temporal, order_table):
    per_device, deg_dev, lat_all = legendre.shape
    latitude_rows_local, time_dev, longitude = direction.shape
    highest = lax.Precision.HIGHEST
    blk, tm = ("blk",), ("x", "core")
    lookup_table = trig_table(order_table, longitude)
    own_orders = lax.dynamic_slice_in_dim(order_table, lax.axis_index(blk) * per_device, per_device)
    own_degrees = lax.axis_index(tm) * deg_dev + jnp.arange(deg_dev, dtype=jnp.int32)
    keep_mask = own_degrees[None, :, None] >= own_orders[:, None, None]
    mask_applied = jnp.where(keep_mask, legendre, jnp.zeros_like(legendre))
    spectra = jnp.einsum("atj,jc->act", direction, lookup_table, precision=highest).astype(BF)
    cycles = lax.all_to_all(
        spectra.reshape(latitude_rows_local, -1), blk, split_axis=1, concat_axis=0, tiled=True
    )
    cycles = cycles.reshape(lat_all, per_device, 2, time_dev)
    full_table = lax.all_gather(mask_applied, tm, axis=1, tiled=True)
    coeffs = jnp.einsum("kla,akct->kclt", full_table, cycles, preferred_element_type=F32)
    coeffs = lax.all_to_all(coeffs, tm, split_axis=2, concat_axis=3, tiled=True)
    mixed = jnp.einsum("ltu,kclu->kclt", temporal, coeffs, precision=highest).astype(BF)
    returned = lax.all_to_all(mixed, tm, split_axis=3, concat_axis=2, tiled=True)
    terms = jnp.einsum("kla,kclt->takc", full_table, returned, preferred_element_type=F32)
    terms = terms.reshape(time_dev, lat_all, per_device * 2)
    column_entries = lax.all_to_all(terms, blk, split_axis=1, concat_axis=2, tiled=True)
    harmonic_synthesis = jnp.einsum("qpo,lo->pql", column_entries, lookup_table, precision=highest)
    product = harmonic_synthesis + noise_var * direction
    every = blk + tm
    norm_now = lax.psum(jnp.sum(residual * residual), every)
    curvature = lax.psum(jnp.sum(direction * product), every)
    step_size = norm_now / curvature
    solution_new = solution + step_size * direction
    residual_new = residual - step_size * product
    norm_next = lax.psum(jnp.sum(residual_new * residual_new), every)
    direction_new = residual_new + norm_next / norm_now * direction
    return (solution_new, residual_new, direction_new)


def swap_halves(v):
    half = LANES // 2
    return jnp.concatenate([v[..., half:], v[..., :half]], axis=-1)


def low_half(shape):
    return lax.broadcasted_iota(jnp.int32, shape, len(shape) - 1) < LANES // 2


def analysis_call(direction4, tables):
    cycles, lo_n, hi_n, length = direction4.shape
    cols = tables[0].shape[0]
    n_tab = len(tables)
    sub = 8
    steps = hi_n // sub
    parts_n = length // LANES

    def kernel(*refs):
        x_refs = refs[:parts_n]
        tab_refs = refs[parts_n : parts_n + n_tab]
        o_refs = refs[parts_n + n_tab : parts_n + 2 * n_tab]
        s_ref = refs[-1]
        h = pl.program_id(0)
        flat = [ref.reshape(cycles * lo_n * sub, LANES) for ref in x_refs]

        def pair(i, carry):
            parts = []
            for ii in range(2):
                for lo in range(lo_n):
                    at = pl.ds(lo * sub + 2 * i + ii, cycles, stride=lo_n * sub)
                    parts.append(jnp.concatenate([ref[at, :].astype(BF) for ref in flat], axis=1))
            x = jnp.concatenate(parts, axis=0)
            for n in range(n_tab):
                y = lax.dot_general(
                    tab_refs[n][...], x, (((1,), (1,)), ((), ())), preferred_element_type=F32
                )
                for ii in range(2):
                    s_ref[n, pl.ds(h * sub + 2 * i + ii, cols, stride=hi_n), :] = y[
                        :, ii * LANES : (ii + 1) * LANES
                    ]
            return carry

        lax.fori_loop(0, sub // 2, pair, 0)

        @pl.when(h == steps - 1)
        def _():
            for n in range(n_tab):
                o_refs[n][...] = s_ref[n].reshape(cols, hi_n, LANES).astype(BF)

    out = jax.ShapeDtypeStruct((cols, hi_n, LANES), BF)
    return pl.pallas_call(
        kernel,
        out_shape=(out,) * n_tab,
        grid=(steps,),
        in_specs=[
            pl.BlockSpec((cycles, lo_n, sub, LANES), lambda h, p=p: (0, 0, h, p))
            for p in range(parts_n)
        ]
        + [pl.BlockSpec((cols, length), lambda h: (0, 0))] * n_tab,
        out_specs=(pl.BlockSpec((cols, hi_n, LANES), lambda h: (0, 0, 0)),) * n_tab,
        scratch_shapes=[pltpu.VMEM((n_tab, cols * hi_n, LANES), F32)],
        compiler_params=pltpu.CompilerParams(vmem_limit_bytes=60 << 20),
        cost_estimate=pl.CostEstimate(
            flops=2 * n_tab * cols * cycles * lo_n * hi_n * length,
            bytes_accessed=direction4.size * 4 + n_tab * cols * length * 2,
            transcendentals=0,
        ),
        name="analysis",
    )(*[direction4] * parts_n, *tables)


def degree_call(scalars, legendre, temporal, gathered, n_x):
    _, deg_dev, lat_all = legendre.shape
    time_all = temporal.shape[-1]
    n_pieces = len(gathered)
    nb, _, chunk_n, hi_n, _ = gathered[0].shape
    time_dev = 2 * hi_n
    kb = 8
    lb = 32
    n1 = chunk_n // kb
    n2 = deg_dev // lb
    pitch = deg_dev + 8
    rows = 2 * time_all
    order_at = 1 + 2 * n_pieces
    row_at = order_at + chunk_n

    def kernel(sc_ref, *refs):
        leg_refs, tmp_ref, refs = refs[:kb], refs[kb], refs[kb + 1 :]
        r_refs = refs[:n_pieces]
        keep_ref, send_ref, c_ref, r_scr, g_scr = refs[n_pieces:]
        step = pl.program_id(0)
        low = low_half((hi_n, LANES))

        def masked(kk, k):
            order = sc_ref[order_at + k]
            degree = sc_ref[0] + lax.broadcasted_iota(jnp.int32, (deg_dev, lat_all), 0)
            values = leg_refs[kk][0]
            return jnp.where(degree >= order, values, jnp.zeros_like(values))

        @pl.when(step < n1)
        def _():
            for kk in range(kb):
                for q in range(n_pieces):
                    base = sc_ref[1 + q] * time_dev
                    for c in range(2):
                        for p in range(nb // 2):
                            even = r_refs[q][2 * p, c, kk]
                            odd = r_refs[q][2 * p + 1, c, kk]
                            for lo in range(2):
                                at = pl.multiple_of(c * time_all + base + lo * hi_n, hi_n)
                                if lo == 0:
                                    v = jnp.where(low, even, swap_halves(odd))
                                else:
                                    v = jnp.where(low, swap_halves(even), odd)
                                r_scr[kk, pl.ds(at, hi_n), p * LANES : (p + 1) * LANES] = v
                k = step * kb + kk
                y = lax.dot_general(
                    masked(kk, k), r_scr[kk], (((1,), (1,)), ((), ())), preferred_element_type=F32
                )
                for c in range(2):
                    at = pl.multiple_of((k * 2 + c) * pitch, 8)
                    c_ref[pl.ds(at, deg_dev), :] = y[:, c * time_all : (c + 1) * time_all]

        @pl.when((step >= n1) & (step < n1 + n2))
        def _():
            for i in range(lb):
                at = (step - n1) * lb + i
                v = c_ref[pl.ds(at, 2 * chunk_n, stride=pitch), :].astype(BF)
                w = tmp_ref[i]
                c_ref[pl.ds(at, 2 * chunk_n, stride=pitch), :] = jnp.dot(
                    v, w, preferred_element_type=F32
                )

        @pl.when(step >= n1 + n2)
        def _():
            for kk in range(kb):
                k = (step - n1 - n2) * kb + kk
                m = masked(kk, k)
                for c in range(2):
                    at = pl.multiple_of((k * 2 + c) * pitch, 8)
                    v = c_ref[pl.ds(at, deg_dev), :].astype(BF)
                    g_scr[kk, c * time_all : (c + 1) * time_all, :] = lax.dot_general(
                        v, m, (((0,), (0,)), ((), ())), preferred_element_type=F32
                    ).astype(BF)
                for q in range(n_pieces):
                    base = sc_ref[1 + n_pieces + q] * time_dev
                    out = keep_ref if q < n_x else send_ref
                    for c in range(2):
                        for p in range(nb // 2):
                            at = pl.multiple_of(c * time_all + base, hi_n)
                            lanes = slice(p * LANES, (p + 1) * LANES)
                            v0 = g_scr[kk, pl.ds(at, hi_n), lanes]
                            v1 = g_scr[kk, pl.ds(at + hi_n, hi_n), lanes]
                            out[q % n_x, 2 * p, c, kk] = jnp.where(low, v0, swap_halves(v1))
                            out[q % n_x, 2 * p + 1, c, kk] = jnp.where(low, swap_halves(v0), v1)

    def leg_spec(kk):
        def index(s, sc):
            step = jnp.where(s < n1, s, jnp.where(s < n1 + n2, n1 - 1, s - n1 - n2))
            return (sc[row_at + step * kb + kk], 0, 0)

        return pl.BlockSpec((1, deg_dev, lat_all), index)

    piece = (nb, 2, chunk_n, hi_n, LANES)
    out_block = pl.BlockSpec(
        (n_x, nb, 2, kb, hi_n, LANES),
        lambda s, sc: (0, 0, 0, jnp.maximum(s - n1 - n2, 0), 0, 0),
    )
    out_shape = jax.ShapeDtypeStruct((n_x,) + piece, BF)
    flops = 4 * chunk_n * deg_dev * lat_all * rows + 2 * deg_dev * 2 * chunk_n * time_all**2
    return pl.pallas_call(
        kernel,
        out_shape=(out_shape, out_shape),
        grid_spec=pltpu.PrefetchScalarGridSpec(
            num_scalar_prefetch=1,
            grid=(n1 + n2 + n1,),
            in_specs=[leg_spec(kk) for kk in range(kb)]
            + [
                pl.BlockSpec(
                    (lb, time_all, time_all),
                    lambda s, sc: (jnp.clip(s - n1, 0, n2 - 1), 0, 0),
                ),
            ]
            + [
                pl.BlockSpec(
                    (nb, 2, kb, hi_n, LANES),
                    lambda s, sc: (0, 0, jnp.minimum(s, n1 - 1), 0, 0),
                )
            ]
            * n_pieces,
            out_specs=(out_block, out_block),
            scratch_shapes=[
                pltpu.VMEM((2 * chunk_n * pitch, time_all), F32),
                pltpu.VMEM((kb, rows, lat_all), BF),
                pltpu.VMEM((kb, rows, lat_all), BF),
            ],
        ),
        compiler_params=pltpu.CompilerParams(vmem_limit_bytes=60 << 20),
        cost_estimate=pl.CostEstimate(
            flops=flops,
            bytes_accessed=4 * chunk_n * deg_dev * lat_all
            + temporal.size * 2
            + 4 * n_pieces * gathered[0].size,
            transcendentals=0,
        ),
        name="degrees",
    )(scalars, *[legendre] * kb, temporal, *gathered)


def synthesis_call(received, tables, previous, fields, scale):
    n_tab = len(received)
    cols, hi_n, _ = received[0].shape
    length = tables[0].shape[-1]
    lo_n = 2
    cycles = LANES // lo_n
    sub = 8
    jb = 512
    batch = 4
    last = previous is not None
    n_grid = 3 if last else 2

    def kernel(*refs):
        rec_refs = refs[:n_tab]
        tab_refs = refs[n_tab : 2 * n_tab]
        grid_refs = refs[2 * n_tab : 2 * n_tab + n_grid]
        o_ref = refs[2 * n_tab + n_grid]
        sum_ref = refs[2 * n_tab + n_grid + 1] if last else None
        s_ref = refs[-1]
        h, j = pl.program_id(0), pl.program_id(1)
        if last:
            p_ref = o_ref.at[h, j]
            d_ref, r_ref = (refs[2 * n_tab + n_grid + n].at[h, j] for n in (2, 3))
        else:
            p_ref = refs[-2]

        @pl.when((h == 0) & (j == 0))
        def _():
            for n in range(n_tab):
                s_ref[n * cols * hi_n : (n + 1) * cols * hi_n, :] = (
                    rec_refs[n][...].astype(F32).reshape(cols * hi_n, LANES)
                )
            if last:
                sum_ref[...] = jnp.zeros_like(sum_ref)

        def some(i, carry):
            y = None
            for n in range(n_tab):
                parts = []
                for ii in range(batch):
                    at = n * cols * hi_n + h * sub + i * batch + ii
                    parts.append(s_ref[pl.ds(at, cols, stride=hi_n), :].astype(BF))
                term = lax.dot_general(
                    jnp.concatenate(parts, axis=1),
                    tab_refs[n][...],
                    (((0,), (0,)), ((), ())),
                    preferred_element_type=F32,
                )
                y = term if y is None else y + term
            y = y * scale
            for ii in range(batch):
                for lo in range(lo_n):
                    at = pl.ds(lo * sub + i * batch + ii, cycles, stride=lo_n * sub)
                    rows = slice((ii * lo_n + lo) * cycles, (ii * lo_n + lo + 1) * cycles)
                    for part in range(jb // LANES):
                        lanes = slice(part * LANES, (part + 1) * LANES)
                        p_ref[part, at, :] = y[rows, lanes]
            return carry

        lax.fori_loop(0, sub // batch, some, 0)
        group = 8

        def finish(i, carry):
            carry = list(carry)
            block = pl.ds(i * group, group)
            for part in range(jb // LANES):
                lanes = slice(part * LANES, (part + 1) * LANES)
                span = group * lo_n * sub
                rows = pl.ds(pl.multiple_of(i * span, span), span)
                p = p_ref[part, rows, :].reshape(group, lo_n, sub, LANES)
                if last:
                    p = p + grid_refs[0][block, :, :, lanes]
                    d = grid_refs[1][block, :, :, lanes]
                    r = grid_refs[2][block, :, :, lanes]
                    for n, term in enumerate((r * r, d * p, r * p, p * p)):
                        carry[n] = carry[n] + jnp.sum(term, axis=(0, 1))
                    for ref, v in ((p_ref, p), (d_ref, d), (r_ref, r)):
                        ref[part, rows, :] = v.reshape(span, LANES)
                else:
                    p = p + grid_refs[0][block, :, :, lanes] * grid_refs[1][block, :, :, lanes]
                    o_ref[block, :, :, lanes] = p
            return tuple(carry)

        zero = (jnp.zeros((sub, LANES), F32),) * 4
        sums = lax.fori_loop(0, cycles // group, finish, zero)
        if last:
            for n in range(4):
                sum_ref[n : n + 1, :] = sum_ref[n : n + 1, :] + jnp.sum(
                    sums[n], axis=0, keepdims=True
                )

    grid_block = pl.BlockSpec((cycles, lo_n, sub, jb), lambda h, j: (0, 0, h, j))
    in_specs = (
        [pl.BlockSpec((cols, hi_n, LANES), lambda h, j: (0, 0, 0))] * n_tab
        + [pl.BlockSpec((cols, jb), lambda h, j: (0, j))] * n_tab
        + [grid_block] * n_grid
    )
    tile_rows = cycles * lo_n * sub
    if last:
        held = pltpu.VMEM((hi_n // sub, length // jb, jb // LANES, tile_rows, LANES), F32)
        whole = pl.BlockSpec(memory_space=pltpu.VMEM)
        out_shape = [held, jax.ShapeDtypeStruct((sub, LANES), F32), held, held]
        out_specs = [whole, pl.BlockSpec((sub, LANES), lambda h, j: (0, 0)), whole, whole]
    else:
        out_shape = [jax.ShapeDtypeStruct((cycles, lo_n, hi_n, length), F32)]
        out_specs = [grid_block]
    grids = ((previous,) if last else ()) + tuple(fields)
    return pl.pallas_call(
        kernel,
        out_shape=tuple(out_shape),
        grid=(hi_n // sub, length // jb),
        in_specs=in_specs,
        out_specs=tuple(out_specs),
        scratch_shapes=([] if last else [pltpu.VMEM((jb // LANES, tile_rows, LANES), F32)])
        + [pltpu.VMEM((n_tab * cols * hi_n, LANES), F32)],
        compiler_params=pltpu.CompilerParams(vmem_limit_bytes=(24 << 20) if last else (60 << 20)),
        cost_estimate=pl.CostEstimate(
            flops=2 * n_tab * cols * LANES * hi_n * length,
            bytes_accessed=4 * cycles * lo_n * hi_n * length * (n_grid + 1),
            transcendentals=0,
        ),
        name="synthesis",
    )(*received, *tables, *grids)


def update_call(sums, solution4, held):
    cycles, lo_n, hi_n, length = solution4.shape
    _, steps_j, parts, _, _ = held[0].shape
    sub, jb = hi_n // held[0].shape[0], length // steps_j
    group = 8
    span = group * lo_n * sub

    n_sums = len(sums)

    def kernel(*refs):
        x_ref, p_ref, r_ref, d_ref, xo_ref, ro_ref, do_ref = refs[n_sums:]
        h, j = pl.program_id(0), pl.program_id(1)
        total = refs[0][...]
        for ref in refs[1:n_sums]:
            total = total + ref[...]
        norm_now, curvature, cross, square = (
            jnp.sum(total[n : n + 1], keepdims=True) for n in range(4)
        )
        step = norm_now / curvature
        norm_next = norm_now - 2.0 * (step * cross) + step * (step * square)
        ratio = norm_next / norm_now

        def some(i, carry):
            block = pl.ds(i * group, group)
            rows = pl.ds(pl.multiple_of(i * span, span), span)
            for part in range(parts):
                lanes = slice(part * LANES, (part + 1) * LANES)
                p, r, d = (
                    ref[h, j, part, rows, :].reshape(group, lo_n, sub, LANES)
                    for ref in (p_ref, r_ref, d_ref)
                )
                xo_ref[block, :, :, lanes] = x_ref[block, :, :, lanes] + step * d
                r = r - step * p
                ro_ref[block, :, :, lanes] = r
                do_ref[block, :, :, lanes] = r + ratio * d
            return carry

        lax.fori_loop(0, cycles // group, some, 0)

    spec = pl.BlockSpec((cycles, lo_n, sub, jb), lambda h, j: (0, 0, h, j))
    size = solution4.size
    return pl.pallas_call(
        kernel,
        out_shape=(jax.ShapeDtypeStruct(solution4.shape, F32),) * 3,
        grid=(hi_n // sub, steps_j),
        in_specs=[pl.BlockSpec(sums[0].shape, lambda h, j: (0, 0))] * n_sums
        + [spec]
        + [pl.BlockSpec(memory_space=pltpu.VMEM)] * 3,
        out_specs=(spec,) * 3,
        compiler_params=pltpu.CompilerParams(vmem_limit_bytes=24 << 20),
        cost_estimate=pl.CostEstimate(
            flops=6 * size, bytes_accessed=16 * size, transcendentals=0
        ),
        name="update",
    )(*sums, solution4, *(pltpu.with_memory_space_constraint(v, pltpu.VMEM) for v in held))


def add_call(values):
    def kernel(*refs):
        total = refs[0][...]
        for ref in refs[1:-1]:
            total = total + ref[...]
        refs[-1][...] = total

    return pl.pallas_call(
        kernel,
        out_shape=jax.ShapeDtypeStruct(values[0].shape, F32),
        compiler_params=pltpu.CompilerParams(vmem_limit_bytes=1 << 20),
        name="add",
    )(*values)


def sum_parts(values, n_blk, n_x, n_core):
    def stage(v, axes, perms):
        return [v] + [lax.ppermute(v, axes, perm) for perm in perms]

    n_tm = n_x * n_core
    tm = [[(i, (i + s) % n_tm) for i in range(n_tm)] for s in range(1, n_tm)]
    pair = [[(i, i ^ 1) for i in range(n_blk)]]
    rest = [[(i, (i + s) % n_blk) for i in range(n_blk)] for s in range(2, n_blk, 2)]
    values = add_call(stage(values, ("x", "core"), tm))
    values = add_call(stage(values, "blk", pair))
    return stage(values, "blk", rest)


def sine_table(phases, length):
    folded = jnp.abs(phases - length // 2) - length // 4
    x = folded.astype(F32) * (2.0 * math.pi / length)
    z = x * x
    value = jnp.full_like(z, -1.0 / math.factorial(11))
    for n in (9, 7, 5, 3, 1):
        value = value * z + (1.0 if n % 4 == 1 else -1.0) / math.factorial(n)
    return value * x


def fast_body(mesh, solution, residual, direction, noise_var, legendre, temporal, order_table):
    per_device, deg_dev, _ = legendre.shape
    cycles, time_dev, longitude = direction.shape
    nb, n_x, n_core = (mesh.shape[name] for name in ("blk", "x", "core"))
    lo_n = LANES // cycles
    hi_n = time_dev // lo_n
    chunk_n = per_device // CHUNKS
    cols = nb * 2 * chunk_n
    blk_i, x_i, core_i = (lax.axis_index(name) for name in ("blk", "x", "core"))
    half = per_device // 2
    halves_of = order_table.reshape(nb, 2, half)
    grouped = jnp.stack([jnp.min(halves_of, axis=1), jnp.max(halves_of, axis=1)])
    own = lax.dynamic_slice_in_dim(halves_of, blk_i, 1)[0]
    slots = jnp.arange(half, dtype=jnp.int32)
    flip = jnp.where(own[0] < own[1], 0, half)
    own_rows = jnp.stack([slots + flip, slots + half - flip])
    own_orders = jnp.stack([jnp.min(own, axis=0), jnp.max(own, axis=0)])
    shape4 = (cycles, lo_n, hi_n, longitude)
    direction4, noise4, residual4 = (v.reshape(shape4) for v in (direction, noise_var, residual))
    quarter = (longitude // 4) * 3

    def table_of(chunk):
        high, start = PLAN[chunk]
        orders = grouped[high][:, start * chunk_n : (start + 1) * chunk_n]
        points = jnp.arange(longitude, dtype=jnp.int32)
        turn = jnp.arange(2, dtype=jnp.int32) * quarter
        phases = orders[:, None, :, None] * points + turn[None, :, None, None]
        return sine_table(phases % longitude, longitude).astype(BF).reshape(cols, longitude)

    forth = [jnp.mod(x_i - s, n_x) * n_core + (core_i + o) % n_core for o in range(2) for s in range(n_x)]
    back = [jnp.mod(x_i + s, n_x) * n_core + (core_i + o) % n_core for o in range(2) for s in range(n_x)]
    base = (x_i * n_core + core_i) * deg_dev
    header = jnp.stack([base] + forth + back).astype(jnp.int32)
    swap = [(i, (i + 1) % n_core) for i in range(n_core)]

    def shift(v, s, keep):
        pairs = [(i, (i + s) % n_x) for i in range(n_x)]
        return lax.ppermute(v, "x", [pair for pair in pairs if keep(*pair)])

    def across(v):
        return lax.all_to_all(v, "blk", split_axis=0, concat_axis=0, tiled=True)

    tables = [table_of(0)]
    spectra = list(analysis_call(direction4, tables))
    piece = (nb, 2, chunk_n, hi_n, LANES)
    tables += [table_of(g) for g in range(1, CHUNKS)]
    spectra += list(analysis_call(direction4, tables[1:]))
    temporal_narrow = temporal.astype(BF)
    received = []
    for g, (high, start) in enumerate(PLAN):

        def forward(source, target):
            return target > 0 or not high

        def backward(source, target):
            return source > 0 or not high

        mine = across(spectra[g].reshape(piece))
        own = [mine] + [shift(mine, s, forward) for s in range(1, n_x)]
        pieces = own + [lax.ppermute(v, "core", swap) for v in own]
        span = slice(start * chunk_n, (start + 1) * chunk_n)
        scalars = jnp.concatenate([header, own_orders[high, span], own_rows[high, span]])
        keep, send = degree_call(scalars, legendre, temporal_narrow, pieces, n_x)
        other = lax.ppermute(send, "core", swap)
        halves = [keep[s].astype(F32) + other[s].astype(F32) for s in range(n_x)]
        halves = [halves[0].astype(BF)] + [v.astype(BF) for v in halves[1:]]
        parts = [shift(halves[s], s, backward) for s in range(1, n_x)]
        total = halves[0].astype(F32)
        for part in parts:
            total = total + part.astype(F32)
        total = total.astype(BF)
        received.append(across(total).reshape(cols, hi_n, LANES))
    scale = 2.0 / longitude
    (partial,) = synthesis_call(received[:-1], tables[:-1], None, (noise4, direction4), scale)
    product, sums, near_d, near_r = synthesis_call(
        received[-1:], tables[-1:], partial, (direction4, residual4), scale
    )
    sums = sum_parts(sums, nb, n_x, n_core)
    out = update_call(sums, solution.reshape(shape4), (product, near_r, near_d))
    return tuple(v.reshape(direction.shape) for v in out)


def solution(mesh):
    n_core = 2 if mesh.shape["tm"] % 2 == 0 else 1
    n_x = mesh.shape["tm"] // n_core
    nb = mesh.shape["blk"]
    inner = Mesh(mesh.devices.reshape(nb, n_x, n_core), ("blk", "x", "core"))
    tm = ("x", "core")

    def body(*args):
        direction, legendre = args[2], args[4]
        cycles, time_dev, longitude = direction.shape
        fits = (
            n_core == 2
            and n_x == 2
            and 2 * cycles == LANES
            and time_dev == 2 * PACK
            and nb % 2 == 0
            and longitude % 512 == 0
            and legendre.shape[0] % (8 * CHUNKS) == 0
            and legendre.shape[1] % PACK == 0
            and legendre.shape[2] % LANES == 0
            and args[5].shape[-1] % LANES == 0
        )
        if fits:
            return fast_body(inner, *args)
        return plain_body(*args)

    grid = P("blk", tm, None)
    return jax.shard_map(
        body,
        mesh=inner,
        in_specs=(grid, grid, grid, grid, grid, P(tm, None, None), P()),
        out_specs=(grid, grid, grid),
        check_vma=False,
    )
```

```python
import math

import jax
import jax.numpy as jnp
from jax import lax
from jax.experimental import pallas as pl
from jax.experimental.pallas import tpu as pltpu
from jax.sharding import Mesh, PartitionSpec as P


LANES = 128
PACK = 16
PLAN = ((0, 0), (1, 0), (1, 1), (0, 1))
TRIPS = ((0,), (1,), (2, 3))
CHUNKS = len(PLAN)
BF = jnp.bfloat16
F32 = jnp.float32


def trig_table(orders, length):
    points = jnp.arange(length, dtype=jnp.int32)
    phases = points[:, None] * orders[None, :] % length
    angles = phases.astype(jnp.float32) * (2.0 * math.pi / length)
    scaling_factor = 1.0 / math.sqrt(length / 2.0)
    stacked = jnp.stack([jnp.cos(angles), jnp.sin(angles)], axis=-1) * scaling_factor
    return stacked.reshape(length, 2 * orders.shape[0])


def plain_body(solution, residual, direction, noise_var, legendre, temporal, order_table):
    per_device, deg_dev, lat_all = legendre.shape
    latitude_rows_local, time_dev, longitude = direction.shape
    highest = lax.Precision.HIGHEST
    blk, tm = ("blk",), ("x", "core")
    lookup_table = trig_table(order_table, longitude)
    own_orders = lax.dynamic_slice_in_dim(order_table, lax.axis_index(blk) * per_device, per_device)
    own_degrees = lax.axis_index(tm) * deg_dev + jnp.arange(deg_dev, dtype=jnp.int32)
    keep_mask = own_degrees[None, :, None] >= own_orders[:, None, None]
    mask_applied = jnp.where(keep_mask, legendre, jnp.zeros_like(legendre))
    spectra = jnp.einsum("atj,jc->act", direction, lookup_table, precision=highest).astype(BF)
    cycles = lax.all_to_all(
        spectra.reshape(latitude_rows_local, -1), blk, split_axis=1, concat_axis=0, tiled=True
    )
    cycles = cycles.reshape(lat_all, per_device, 2, time_dev)
    full_table = lax.all_gather(mask_applied, tm, axis=1, tiled=True)
    coeffs = jnp.einsum("kla,akct->kclt", full_table, cycles, preferred_element_type=F32)
    coeffs = lax.all_to_all(coeffs, tm, split_axis=2, concat_axis=3, tiled=True)
    mixed = jnp.einsum("ltu,kclu->kclt", temporal, coeffs, precision=highest).astype(BF)
    returned = lax.all_to_all(mixed, tm, split_axis=3, concat_axis=2, tiled=True)
    terms = jnp.einsum("kla,kclt->takc", full_table, returned, preferred_element_type=F32)
    terms = terms.reshape(time_dev, lat_all, per_device * 2)
    column_entries = lax.all_to_all(terms, blk, split_axis=1, concat_axis=2, tiled=True)
    harmonic_synthesis = jnp.einsum("qpo,lo->pql", column_entries, lookup_table, precision=highest)
    product = harmonic_synthesis + noise_var * direction
    every = blk + tm
    norm_now = lax.psum(jnp.sum(residual * residual), every)
    curvature = lax.psum(jnp.sum(direction * product), every)
    step_size = norm_now / curvature
    solution_new = solution + step_size * direction
    residual_new = residual - step_size * product
    norm_next = lax.psum(jnp.sum(residual_new * residual_new), every)
    direction_new = residual_new + norm_next / norm_now * direction
    return (solution_new, residual_new, direction_new)


def swap_halves(v):
    half = LANES // 2
    return jnp.concatenate([v[..., half:], v[..., :half]], axis=-1)


def low_half(shape):
    return lax.broadcasted_iota(jnp.int32, shape, len(shape) - 1) < LANES // 2


def analysis_call(direction4, tables, groups, nb):
    cycles, lo_n, hi_n, length = direction4.shape
    cols = tables[0].shape[0]
    n_tab = len(tables)
    sub = 8
    steps = hi_n // sub
    parts_n = length // LANES

    def kernel(*refs):
        x_refs = refs[:parts_n]
        tab_refs = refs[parts_n : parts_n + n_tab]
        o_refs = refs[parts_n + n_tab : -1]
        s_ref = refs[-1]
        h = pl.program_id(0)
        flat = [ref.reshape(cycles * lo_n * sub, LANES) for ref in x_refs]

        def pair(i, carry):
            parts = []
            for ii in range(2):
                for lo in range(lo_n):
                    at = pl.ds(lo * sub + 2 * i + ii, cycles, stride=lo_n * sub)
                    parts.append(jnp.concatenate([ref[at, :].astype(BF) for ref in flat], axis=1))
            x = jnp.concatenate(parts, axis=0)
            for n in range(n_tab):
                y = lax.dot_general(
                    tab_refs[n][...], x, (((1,), (1,)), ((), ())), preferred_element_type=F32
                )
                for ii in range(2):
                    s_ref[n, pl.ds(h * sub + 2 * i + ii, cols, stride=hi_n), :] = y[
                        :, ii * LANES : (ii + 1) * LANES
                    ]
            return carry

        lax.fori_loop(0, sub // 2, pair, 0)

        @pl.when(h == steps - 1)
        def _():
            n = 0
            for ref, count in zip(o_refs, groups):
                for slot in range(count):
                    rows = s_ref[n].reshape(nb, cols // nb, hi_n, LANES)
                    ref[:, slot] = rows.astype(BF)
                    n += 1

    shapes = [(nb, count, cols // nb, hi_n, LANES) for count in groups]
    return pl.pallas_call(
        kernel,
        out_shape=tuple(jax.ShapeDtypeStruct(shape, BF) for shape in shapes),
        grid=(steps,),
        in_specs=[
            pl.BlockSpec((cycles, lo_n, sub, LANES), lambda h, p=p: (0, 0, h, p))
            for p in range(parts_n)
        ]
        + [pl.BlockSpec((cols, length), lambda h: (0, 0))] * n_tab,
        out_specs=tuple(pl.BlockSpec(shape, lambda h: (0,) * 5) for shape in shapes),
        scratch_shapes=[pltpu.VMEM((n_tab, cols * hi_n, LANES), F32)],
        compiler_params=pltpu.CompilerParams(vmem_limit_bytes=60 << 20),
        cost_estimate=pl.CostEstimate(
            flops=2 * n_tab * cols * cycles * lo_n * hi_n * length,
            bytes_accessed=direction4.size * 4 + n_tab * cols * length * 2,
            transcendentals=0,
        ),
        name="analysis",
    )(*[direction4] * parts_n, *tables)


def degree_call(scalars, legendre, temporal, gathered, n_x):
    _, deg_dev, lat_all = legendre.shape
    time_all = temporal.shape[-1]
    n_pieces = len(gathered)
    nb, _, chunk_n, hi_n, _ = gathered[0].shape
    time_dev = 2 * hi_n
    kb = 8
    lb = 32
    n1 = chunk_n // kb
    n2 = deg_dev // lb
    pitch = deg_dev + 8
    rows = 2 * time_all
    order_at = 1 + 2 * n_pieces
    row_at = order_at + chunk_n

    def kernel(sc_ref, *refs):
        leg_refs, tmp_ref, refs = refs[:kb], refs[kb], refs[kb + 1 :]
        r_refs = refs[:n_pieces]
        keep_ref, send_ref, c_ref, r_scr, g_scr = refs[n_pieces:]
        step = pl.program_id(0)
        low = low_half((hi_n, LANES))

        def masked(kk, k):
            order = sc_ref[order_at + k]
            degree = sc_ref[0] + lax.broadcasted_iota(jnp.int32, (deg_dev, lat_all), 0)
            values = leg_refs[kk][0]
            return jnp.where(degree >= order, values, jnp.zeros_like(values))

        @pl.when(step < n1)
        def _():
            for kk in range(kb):
                for q in range(n_pieces):
                    base = sc_ref[1 + q] * time_dev
                    for c in range(2):
                        for p in range(nb // 2):
                            even = r_refs[q][2 * p, c, kk]
                            odd = r_refs[q][2 * p + 1, c, kk]
                            for lo in range(2):
                                at = pl.multiple_of(c * time_all + base + lo * hi_n, hi_n)
                                if lo == 0:
                                    v = jnp.where(low, even, swap_halves(odd))
                                else:
                                    v = jnp.where(low, swap_halves(even), odd)
                                r_scr[kk, pl.ds(at, hi_n), p * LANES : (p + 1) * LANES] = v
                k = step * kb + kk
                y = lax.dot_general(
                    masked(kk, k), r_scr[kk], (((1,), (1,)), ((), ())), preferred_element_type=F32
                )
                for c in range(2):
                    at = pl.multiple_of((k * 2 + c) * pitch, 8)
                    c_ref[pl.ds(at, deg_dev), :] = y[:, c * time_all : (c + 1) * time_all]

        @pl.when((step >= n1) & (step < n1 + n2))
        def _():
            for i in range(lb):
                at = (step - n1) * lb + i
                v = c_ref[pl.ds(at, 2 * chunk_n, stride=pitch), :].astype(BF)
                w = tmp_ref[i]
                c_ref[pl.ds(at, 2 * chunk_n, stride=pitch), :] = jnp.dot(
                    v, w, preferred_element_type=F32
                )

        @pl.when(step >= n1 + n2)
        def _():
            for kk in range(kb):
                k = (step - n1 - n2) * kb + kk
                m = masked(kk, k)
                for c in range(2):
                    at = pl.multiple_of((k * 2 + c) * pitch, 8)
                    v = c_ref[pl.ds(at, deg_dev), :].astype(BF)
                    g_scr[kk, c * time_all : (c + 1) * time_all, :] = lax.dot_general(
                        v, m, (((0,), (0,)), ((), ())), preferred_element_type=F32
                    ).astype(BF)
                for q in range(n_pieces):
                    base = sc_ref[1 + n_pieces + q] * time_dev
                    out = keep_ref if q < n_x else send_ref
                    for c in range(2):
                        for p in range(nb // 2):
                            at = pl.multiple_of(c * time_all + base, hi_n)
                            lanes = slice(p * LANES, (p + 1) * LANES)
                            v0 = g_scr[kk, pl.ds(at, hi_n), lanes]
                            v1 = g_scr[kk, pl.ds(at + hi_n, hi_n), lanes]
                            out[q % n_x, 2 * p, c, kk] = jnp.where(low, v0, swap_halves(v1))
                            out[q % n_x, 2 * p + 1, c, kk] = jnp.where(low, swap_halves(v0), v1)

    def leg_spec(kk):
        def index(s, sc):
            step = jnp.where(s < n1, s, jnp.where(s < n1 + n2, n1 - 1, s - n1 - n2))
            return (sc[row_at + step * kb + kk], 0, 0)

        return pl.BlockSpec((1, deg_dev, lat_all), index)

    piece = (nb, 2, chunk_n, hi_n, LANES)
    out_block = pl.BlockSpec(
        (n_x, nb, 2, kb, hi_n, LANES),
        lambda s, sc: (0, 0, 0, jnp.maximum(s - n1 - n2, 0), 0, 0),
    )
    out_shape = jax.ShapeDtypeStruct((n_x,) + piece, BF)
    flops = 4 * chunk_n * deg_dev * lat_all * rows + 2 * deg_dev * 2 * chunk_n * time_all**2
    return pl.pallas_call(
        kernel,
        out_shape=(out_shape, out_shape),
        grid_spec=pltpu.PrefetchScalarGridSpec(
            num_scalar_prefetch=1,
            grid=(n1 + n2 + n1,),
            in_specs=[leg_spec(kk) for kk in range(kb)]
            + [
                pl.BlockSpec(
                    (lb, time_all, time_all),
                    lambda s, sc: (jnp.clip(s - n1, 0, n2 - 1), 0, 0),
                ),
            ]
            + [
                pl.BlockSpec(
                    (nb, 2, kb, hi_n, LANES),
                    lambda s, sc: (0, 0, jnp.minimum(s, n1 - 1), 0, 0),
                )
            ]
            * n_pieces,
            out_specs=(out_block, out_block),
            scratch_shapes=[
                pltpu.VMEM((2 * chunk_n * pitch, time_all), F32),
                pltpu.VMEM((kb, rows, lat_all), BF),
                pltpu.VMEM((kb, rows, lat_all), BF),
            ],
        ),
        compiler_params=pltpu.CompilerParams(vmem_limit_bytes=60 << 20),
        cost_estimate=pl.CostEstimate(
            flops=flops,
            bytes_accessed=4 * chunk_n * deg_dev * lat_all
            + temporal.size * 2
            + 4 * n_pieces * gathered[0].size,
            transcendentals=0,
        ),
        name="degrees",
    )(scalars, *[legendre] * kb, temporal, *gathered)


def synthesis_call(received, tables, previous, fields, scale):
    n_tab = len(received)
    cols, hi_n, _ = received[0].shape
    length = tables[0].shape[-1]
    lo_n = 2
    cycles = LANES // lo_n
    sub = 8
    jb = 512
    batch = 4
    last = previous is not None
    n_grid = 4 if last else 2

    def kernel(*refs):
        rec_refs = refs[:n_tab]
        tab_refs = refs[n_tab : 2 * n_tab]
        grid_refs = refs[2 * n_tab : 2 * n_tab + n_grid]
        o_ref = refs[2 * n_tab + n_grid]
        sum_ref = refs[2 * n_tab + n_grid + 1] if last else None
        s_ref = refs[-1]
        h, j = pl.program_id(0), pl.program_id(1)
        if last:
            p_ref = o_ref.at[h, j]
            near_refs = refs[2 * n_tab + n_grid + 2 : 2 * n_tab + n_grid + 5]
            d_ref, r_ref = (ref.at[h, j] for ref in near_refs[:2])
            sem = refs[-2]

            def fetch(n, hh, jj):
                source = grid_refs[1 + n].at[
                    :, :, hh * sub : (hh + 1) * sub, jj * jb : (jj + 1) * jb
                ]
                return pltpu.make_async_copy(source, near_refs[n].at[hh, jj], sem.at[n, hh, jj])

            spots = [(hh, jj) for hh in range(hi_n // sub) for jj in range(length // jb)]

            @pl.when((h == 0) & (j == 0))
            def _():
                for n in (0, 1):
                    fetch(n, 0, 0).start()
                for spot in spots[1:]:
                    for n in (0, 1):
                        fetch(n, *spot).start()
                for spot in spots:
                    fetch(2, *spot).start()
        else:
            p_ref = refs[-2]

        @pl.when((h == 0) & (j == 0))
        def _():
            for n in range(n_tab):
                s_ref[n * cols * hi_n : (n + 1) * cols * hi_n, :] = (
                    rec_refs[n][...].astype(F32).reshape(cols * hi_n, LANES)
                )
            if last:
                sum_ref[...] = jnp.zeros_like(sum_ref)

        def some(i, carry):
            y = None
            for n in range(n_tab):
                parts = []
                for ii in range(batch):
                    at = n * cols * hi_n + h * sub + i * batch + ii
                    parts.append(s_ref[pl.ds(at, cols, stride=hi_n), :].astype(BF))
                term = lax.dot_general(
                    jnp.concatenate(parts, axis=1),
                    tab_refs[n][...],
                    (((0,), (0,)), ((), ())),
                    preferred_element_type=F32,
                )
                y = term if y is None else y + term
            y = y * scale
            for ii in range(batch):
                for lo in range(lo_n):
                    at = pl.ds(lo * sub + i * batch + ii, cycles, stride=lo_n * sub)
                    rows = slice((ii * lo_n + lo) * cycles, (ii * lo_n + lo + 1) * cycles)
                    for part in range(jb // LANES):
                        lanes = slice(part * LANES, (part + 1) * LANES)
                        p_ref[part, at, :] = y[rows, lanes]
            return carry

        lax.fori_loop(0, sub // batch, some, 0)
        if last:
            for hh, jj in spots:

                @pl.when((h == hh) & (j == jj))
                def _():
                    for n in (0, 1):
                        fetch(n, hh, jj).wait()

            @pl.when((h == spots[-1][0]) & (j == spots[-1][1]))
            def _():
                for spot in spots:
                    fetch(2, *spot).wait()

        group = 8

        def finish(i, carry):
            carry = list(carry)
            block = pl.ds(i * group, group)
            for part in range(jb // LANES):
                lanes = slice(part * LANES, (part + 1) * LANES)
                span = group * lo_n * sub
                rows = pl.ds(pl.multiple_of(i * span, span), span)
                p = p_ref[part, rows, :].reshape(group, lo_n, sub, LANES)
                if last:
                    p = p + grid_refs[0][block, :, :, lanes]
                    d = d_ref[block, :, :, lanes]
                    r = r_ref[block, :, :, lanes]
                    for n, term in enumerate((r * r, d * p, r * p, p * p)):
                        carry[n] = carry[n] + jnp.sum(term, axis=(0, 1))
                    p_ref[part, rows, :] = p.reshape(span, LANES)
                else:
                    p = p + grid_refs[0][block, :, :, lanes] * grid_refs[1][block, :, :, lanes]
                    o_ref[block, :, :, lanes] = p
            return tuple(carry)

        zero = (jnp.zeros((sub, LANES), F32),) * 4
        sums = lax.fori_loop(0, cycles // group, finish, zero)
        if last:
            for n in range(4):
                sum_ref[n : n + 1, :] = sum_ref[n : n + 1, :] + jnp.sum(
                    sums[n], axis=0, keepdims=True
                )

    grid_block = pl.BlockSpec((cycles, lo_n, sub, jb), lambda h, j: (0, 0, h, j))
    in_specs = (
        [pl.BlockSpec((cols, hi_n, LANES), lambda h, j: (0, 0, 0))] * n_tab
        + [pl.BlockSpec((cols, jb), lambda h, j: (0, j))] * n_tab
        + ([grid_block] + [pl.BlockSpec(memory_space=pltpu.HBM)] * 3 if last else [grid_block] * 2)
    )
    tile_rows = cycles * lo_n * sub
    if last:
        held = pltpu.VMEM((hi_n // sub, length // jb, jb // LANES, tile_rows, LANES), F32)
        whole = pl.BlockSpec(memory_space=pltpu.VMEM)
        steps = (hi_n // sub, length // jb)
        near = pltpu.VMEM(steps + (cycles, lo_n, sub, jb), F32)
        out_shape = [held, jax.ShapeDtypeStruct((sub, LANES), F32)] + [near] * 3
        out_specs = [whole, pl.BlockSpec((sub, LANES), lambda h, j: (0, 0))] + [whole] * 3
    else:
        out_shape = [jax.ShapeDtypeStruct((cycles, lo_n, hi_n, length), F32)]
        out_specs = [grid_block]
    grids = ((previous,) if last else ()) + tuple(fields)
    return pl.pallas_call(
        kernel,
        out_shape=tuple(out_shape),
        grid=(hi_n // sub, length // jb),
        in_specs=in_specs,
        out_specs=tuple(out_specs),
        scratch_shapes=[
            pltpu.SemaphoreType.DMA((3, hi_n // sub, length // jb))
            if last
            else pltpu.VMEM((jb // LANES, tile_rows, LANES), F32)
        ]
        + [pltpu.VMEM((n_tab * cols * hi_n, LANES), F32)],
        compiler_params=pltpu.CompilerParams(vmem_limit_bytes=(16 << 20) if last else (60 << 20)),
        cost_estimate=pl.CostEstimate(
            flops=2 * n_tab * cols * LANES * hi_n * length,
            bytes_accessed=4 * cycles * lo_n * hi_n * length * (n_grid + 1),
            transcendentals=0,
        ),
        name="synthesis",
    )(*received, *tables, *grids)


def update_call(sums, held):
    steps_h, steps_j, cycles, lo_n, sub, jb = held[1].shape
    parts = jb // LANES
    shape4 = (cycles, lo_n, steps_h * sub, steps_j * jb)
    group = 8
    span = group * lo_n * sub

    n_sums = len(sums)

    def kernel(*refs):
        p_ref, d_ref, r_ref, x_ref, xo_ref, ro_ref, do_ref = refs[n_sums:]
        h, j = pl.program_id(0), pl.program_id(1)
        total = refs[0][...]
        for ref in refs[1:n_sums]:
            total = total + ref[...]
        norm_now, curvature, cross, square = (
            jnp.sum(total[n : n + 1], keepdims=True) for n in range(4)
        )
        step = norm_now / curvature
        norm_next = norm_now - 2.0 * (step * cross) + step * (step * square)
        ratio = norm_next / norm_now

        def some(i, carry):
            block = pl.ds(i * group, group)
            rows = pl.ds(pl.multiple_of(i * span, span), span)
            for part in range(parts):
                lanes = slice(part * LANES, (part + 1) * LANES)
                p = p_ref[h, j, part, rows, :].reshape(group, lo_n, sub, LANES)
                d, r, x = (ref[h, j, block, :, :, lanes] for ref in (d_ref, r_ref, x_ref))
                xo_ref[block, :, :, lanes] = x + step * d
                r = r - step * p
                ro_ref[block, :, :, lanes] = r
                do_ref[block, :, :, lanes] = r + ratio * d
            return carry

        lax.fori_loop(0, cycles // group, some, 0)

    spec = pl.BlockSpec((cycles, lo_n, sub, jb), lambda h, j: (0, 0, h, j))
    size = math.prod(shape4)
    return pl.pallas_call(
        kernel,
        out_shape=(jax.ShapeDtypeStruct(shape4, F32),) * 3,
        grid=(steps_h, steps_j),
        in_specs=[pl.BlockSpec(sums[0].shape, lambda h, j: (0, 0))] * n_sums
        + [pl.BlockSpec(memory_space=pltpu.VMEM)] * 4,
        out_specs=(spec,) * 3,
        compiler_params=pltpu.CompilerParams(vmem_limit_bytes=16 << 20),
        cost_estimate=pl.CostEstimate(
            flops=6 * size, bytes_accessed=12 * size, transcendentals=0
        ),
        name="update",
    )(*sums, *(pltpu.with_memory_space_constraint(v, pltpu.VMEM) for v in held))


def add_call(values):
    def kernel(*refs):
        total = refs[0][...]
        for ref in refs[1:-1]:
            total = total + ref[...]
        refs[-1][...] = total

    return pl.pallas_call(
        kernel,
        out_shape=jax.ShapeDtypeStruct(values[0].shape, F32),
        compiler_params=pltpu.CompilerParams(vmem_limit_bytes=1 << 20),
        name="add",
    )(*values)


def sum_parts(values, n_blk, n_x, n_core):
    def stage(v, axes, perms):
        return [v] + [lax.ppermute(v, axes, perm) for perm in perms]

    n_tm = n_x * n_core
    tm = [[(i, (i + s) % n_tm) for i in range(n_tm)] for s in range(1, n_tm)]
    pair = [[(i, i ^ 1) for i in range(n_blk)]]
    rest = [[(i, (i + s) % n_blk) for i in range(n_blk)] for s in range(2, n_blk, 2)]
    values = add_call(stage(values, ("x", "core"), tm))
    values = add_call(stage(values, "blk", pair))
    return stage(values, "blk", rest)


def sine_table(phases, length):
    folded = jnp.abs(phases - length // 2) - length // 4
    x = folded.astype(F32) * (2.0 * math.pi / length)
    z = x * x
    value = jnp.full_like(z, -1.0 / math.factorial(11))
    for n in (9, 7, 5, 3, 1):
        value = value * z + (1.0 if n % 4 == 1 else -1.0) / math.factorial(n)
    return value * x


def fast_body(mesh, solution, residual, direction, noise_var, legendre, temporal, order_table):
    per_device, deg_dev, _ = legendre.shape
    cycles, time_dev, longitude = direction.shape
    nb, n_x, n_core = (mesh.shape[name] for name in ("blk", "x", "core"))
    lo_n = LANES // cycles
    hi_n = time_dev // lo_n
    chunk_n = per_device // CHUNKS
    cols = nb * 2 * chunk_n
    blk_i, x_i, core_i = (lax.axis_index(name) for name in ("blk", "x", "core"))
    half = per_device // 2
    halves_of = order_table.reshape(nb, 2, half)
    grouped = jnp.stack([jnp.min(halves_of, axis=1), jnp.max(halves_of, axis=1)])
    own = lax.dynamic_slice_in_dim(halves_of, blk_i, 1)[0]
    slots = jnp.arange(half, dtype=jnp.int32)
    flip = jnp.where(own[0] < own[1], 0, half)
    own_rows = jnp.stack([slots + flip, slots + half - flip])
    own_orders = jnp.stack([jnp.min(own, axis=0), jnp.max(own, axis=0)])
    shape4 = (cycles, lo_n, hi_n, longitude)
    fields = (solution, residual, direction, noise_var)
    solution4, residual4, direction4, noise4 = (v.reshape(shape4) for v in fields)
    quarter = (longitude // 4) * 3

    def table_of(chunk, grouped):
        high, start = PLAN[chunk]
        orders = grouped[high][:, start * chunk_n : (start + 1) * chunk_n]
        points = jnp.arange(longitude, dtype=jnp.int32)
        turn = jnp.arange(2, dtype=jnp.int32) * quarter
        phases = orders[:, None, :, None] * points + turn[None, :, None, None]
        whole = longitude & (longitude - 1) == 0
        phases = phases & (longitude - 1) if whole else phases % longitude
        return sine_table(phases, longitude).astype(BF).reshape(cols, longitude)

    forth = [jnp.mod(x_i - s, n_x) * n_core + (core_i + o) % n_core for o in range(2) for s in range(n_x)]
    back = [jnp.mod(x_i + s, n_x) * n_core + (core_i + o) % n_core for o in range(2) for s in range(n_x)]
    base = (x_i * n_core + core_i) * deg_dev
    header = jnp.stack([base] + forth + back).astype(jnp.int32)
    swap = [(i, (i + 1) % n_core) for i in range(n_core)]

    def shift(v, s, keep):
        pairs = [(i, (i + s) % n_x) for i in range(n_x)]
        return lax.ppermute(v, "x", [pair for pair in pairs if keep(*pair)])

    def across(v):
        return lax.all_to_all(v, "blk", split_axis=0, concat_axis=0, tiled=True)

    tables = [table_of(0, grouped)]
    spectra = list(analysis_call(direction4, tables, (1,), nb))
    piece = (nb, 2, chunk_n, hi_n, LANES)
    later, spectra[0] = lax.optimization_barrier((grouped, spectra[0]))
    tables += [table_of(g, later) for g in range(1, CHUNKS)]
    counts = tuple(len(trip) for trip in TRIPS[1:])
    spectra += list(analysis_call(direction4, tables[1:], counts, nb))
    temporal_narrow = temporal.astype(BF)
    arrived = []
    for n, trip in enumerate(TRIPS):
        moved = across(spectra[n])
        arrived += [moved[:, slot].reshape(piece) for slot in range(len(trip))]
    received = []
    for g, (high, start) in enumerate(PLAN):

        def forward(source, target):
            return target > 0 or not high

        def backward(source, target):
            return source > 0 or not high

        mine = arrived[g]
        own = [mine] + [shift(mine, s, forward) for s in range(1, n_x)]
        pieces = own + [lax.ppermute(v, "core", swap) for v in own]
        span = slice(start * chunk_n, (start + 1) * chunk_n)
        scalars = jnp.concatenate([header, own_orders[high, span], own_rows[high, span]])
        keep, send = degree_call(scalars, legendre, temporal_narrow, pieces, n_x)
        other = lax.ppermute(send, "core", swap)
        halves = [keep[s].astype(F32) + other[s].astype(F32) for s in range(n_x)]
        halves = [halves[0].astype(BF)] + [v.astype(BF) for v in halves[1:]]
        parts = [shift(halves[s], s, backward) for s in range(1, n_x)]
        total = halves[0].astype(F32)
        for part in parts:
            total = total + part.astype(F32)
        total = total.astype(BF)
        received.append(across(total).reshape(cols, hi_n, LANES))
    scale = 2.0 / longitude
    (partial,) = synthesis_call(received[:-1], tables[:-1], None, (noise4, direction4), scale)
    product, sums, *near = synthesis_call(
        received[-1:], tables[-1:], partial, (direction4, residual4, solution4), scale
    )
    sums = sum_parts(sums, nb, n_x, n_core)
    out = update_call(sums, (product, *near))
    return tuple(v.reshape(direction.shape) for v in out)


def solution(mesh):
    n_core = 2 if mesh.shape["tm"] % 2 == 0 else 1
    n_x = mesh.shape["tm"] // n_core
    nb = mesh.shape["blk"]
    inner = Mesh(mesh.devices.reshape(nb, n_x, n_core), ("blk", "x", "core"))
    tm = ("x", "core")

    def body(*args):
        direction, legendre = args[2], args[4]
        cycles, time_dev, longitude = direction.shape
        fits = (
            n_core == 2
            and n_x == 2
            and 2 * cycles == LANES
            and time_dev == 2 * PACK
            and nb % 2 == 0
            and longitude % 512 == 0
            and legendre.shape[0] % (8 * CHUNKS) == 0
            and legendre.shape[1] % PACK == 0
            and legendre.shape[2] % LANES == 0
            and args[5].shape[-1] % LANES == 0
        )
        if fits:
            return fast_body(inner, *args)
        return plain_body(*args)

    grid = P("blk", tm, None)
    return jax.shard_map(
        body,
        mesh=inner,
        in_specs=(grid, grid, grid, grid, grid, P(tm, None, None), P()),
        out_specs=(grid, grid, grid),
        check_vma=False,
    )
```

```python
import math

import jax
import jax.numpy as jnp
from jax import lax
from jax.experimental import pallas as pl
from jax.experimental.pallas import tpu as pltpu
from jax.sharding import Mesh, PartitionSpec as P


LANES = 128
PACK = 16
PLAN = ((0, 0), (1, 0), (1, 1), (0, 1))
TRIPS = ((0,), (1,), (2, 3))
CHUNKS = len(PLAN)
BF = jnp.bfloat16
F32 = jnp.float32


def trig_table(orders, length):
    points = jnp.arange(length, dtype=jnp.int32)
    phases = points[:, None] * orders[None, :] % length
    angles = phases.astype(jnp.float32) * (2.0 * math.pi / length)
    scaling_factor = 1.0 / math.sqrt(length / 2.0)
    stacked = jnp.stack([jnp.cos(angles), jnp.sin(angles)], axis=-1) * scaling_factor
    return stacked.reshape(length, 2 * orders.shape[0])


def plain_body(solution, residual, direction, noise_var, legendre, temporal, order_table):
    per_device, deg_dev, lat_all = legendre.shape
    latitude_rows_local, time_dev, longitude = direction.shape
    highest = lax.Precision.HIGHEST
    blk, tm = ("blk",), ("x", "core")
    lookup_table = trig_table(order_table, longitude)
    own_orders = lax.dynamic_slice_in_dim(order_table, lax.axis_index(blk) * per_device, per_device)
    own_degrees = lax.axis_index(tm) * deg_dev + jnp.arange(deg_dev, dtype=jnp.int32)
    keep_mask = own_degrees[None, :, None] >= own_orders[:, None, None]
    mask_applied = jnp.where(keep_mask, legendre, jnp.zeros_like(legendre))
    spectra = jnp.einsum("atj,jc->act", direction, lookup_table, precision=highest).astype(BF)
    cycles = lax.all_to_all(
        spectra.reshape(latitude_rows_local, -1), blk, split_axis=1, concat_axis=0, tiled=True
    )
    cycles = cycles.reshape(lat_all, per_device, 2, time_dev)
    full_table = lax.all_gather(mask_applied, tm, axis=1, tiled=True)
    coeffs = jnp.einsum("kla,akct->kclt", full_table, cycles, preferred_element_type=F32)
    coeffs = lax.all_to_all(coeffs, tm, split_axis=2, concat_axis=3, tiled=True)
    mixed = jnp.einsum("ltu,kclu->kclt", temporal, coeffs, precision=highest).astype(BF)
    returned = lax.all_to_all(mixed, tm, split_axis=3, concat_axis=2, tiled=True)
    terms = jnp.einsum("kla,kclt->takc", full_table, returned, preferred_element_type=F32)
    terms = terms.reshape(time_dev, lat_all, per_device * 2)
    column_entries = lax.all_to_all(terms, blk, split_axis=1, concat_axis=2, tiled=True)
    harmonic_synthesis = jnp.einsum("qpo,lo->pql", column_entries, lookup_table, precision=highest)
    product = harmonic_synthesis + noise_var * direction
    every = blk + tm
    norm_now = lax.psum(jnp.sum(residual * residual), every)
    curvature = lax.psum(jnp.sum(direction * product), every)
    step_size = norm_now / curvature
    solution_new = solution + step_size * direction
    residual_new = residual - step_size * product
    norm_next = lax.psum(jnp.sum(residual_new * residual_new), every)
    direction_new = residual_new + norm_next / norm_now * direction
    return (solution_new, residual_new, direction_new)


def swap_halves(v):
    half = LANES // 2
    return jnp.concatenate([v[..., half:], v[..., :half]], axis=-1)


def low_half(shape):
    return lax.broadcasted_iota(jnp.int32, shape, len(shape) - 1) < LANES // 2


def analysis_call(direction4, tables, groups, nb):
    cycles, lo_n, hi_n, length = direction4.shape
    cols = tables[0].shape[0]
    n_tab = len(tables)
    sub = 8
    steps = hi_n // sub
    parts_n = length // LANES

    def kernel(*refs):
        x_refs = refs[:parts_n]
        tab_refs = refs[parts_n : parts_n + n_tab]
        o_refs = refs[parts_n + n_tab : -1]
        s_ref = refs[-1]
        h = pl.program_id(0)
        flat = [ref.reshape(cycles * lo_n * sub, LANES) for ref in x_refs]

        def pair(i, carry):
            parts = []
            for ii in range(2):
                for lo in range(lo_n):
                    at = pl.ds(lo * sub + 2 * i + ii, cycles, stride=lo_n * sub)
                    parts.append(jnp.concatenate([ref[at, :].astype(BF) for ref in flat], axis=1))
            x = jnp.concatenate(parts, axis=0)
            for n in range(n_tab):
                y = lax.dot_general(
                    tab_refs[n][...], x, (((1,), (1,)), ((), ())), preferred_element_type=F32
                )
                for ii in range(2):
                    s_ref[n, pl.ds(h * sub + 2 * i + ii, cols, stride=hi_n), :] = y[
                        :, ii * LANES : (ii + 1) * LANES
                    ]
            return carry

        lax.fori_loop(0, sub // 2, pair, 0)

        @pl.when(h == steps - 1)
        def _():
            n = 0
            for ref, count in zip(o_refs, groups):
                for slot in range(count):
                    rows = s_ref[n].reshape(nb, cols // nb, hi_n, LANES)
                    ref[:, slot] = rows.astype(BF)
                    n += 1

    shapes = [(nb, count, cols // nb, hi_n, LANES) for count in groups]
    return pl.pallas_call(
        kernel,
        out_shape=tuple(jax.ShapeDtypeStruct(shape, BF) for shape in shapes),
        grid=(steps,),
        in_specs=[
            pl.BlockSpec((cycles, lo_n, sub, LANES), lambda h, p=p: (0, 0, h, p))
            for p in range(parts_n)
        ]
        + [pl.BlockSpec((cols, length), lambda h: (0, 0))] * n_tab,
        out_specs=tuple(pl.BlockSpec(shape, lambda h: (0,) * 5) for shape in shapes),
        scratch_shapes=[pltpu.VMEM((n_tab, cols * hi_n, LANES), F32)],
        compiler_params=pltpu.CompilerParams(vmem_limit_bytes=60 << 20),
        cost_estimate=pl.CostEstimate(
            flops=2 * n_tab * cols * cycles * lo_n * hi_n * length,
            bytes_accessed=direction4.size * 4 + n_tab * cols * length * 2,
            transcendentals=0,
        ),
        name="analysis",
    )(*[direction4] * parts_n, *tables)


def degree_call(scalars, legendre, temporal, gathered):
    _, deg_dev, lat_all = legendre.shape
    time_all = temporal.shape[-1]
    n_pieces = len(gathered)
    nb, _, chunk_n, hi_n, _ = gathered[0].shape
    time_dev = 2 * hi_n
    kb = 8
    lb = 32
    n1 = chunk_n // kb
    n2 = deg_dev // lb
    pitch = deg_dev + 8
    rows = 2 * time_all
    order_at = 1 + 2 * n_pieces
    row_at = order_at + chunk_n

    def kernel(sc_ref, *refs):
        leg_refs, tmp_ref, refs = refs[:kb], refs[kb], refs[kb + 1 :]
        r_refs = refs[:n_pieces]
        out_refs = refs[n_pieces : 2 * n_pieces]
        c_ref, r_scr, g_scr = refs[2 * n_pieces :]
        step = pl.program_id(0)
        low = low_half((hi_n, LANES))

        def masked(kk, k):
            order = sc_ref[order_at + k]
            degree = sc_ref[0] + lax.broadcasted_iota(jnp.int32, (deg_dev, lat_all), 0)
            values = leg_refs[kk][0]
            return jnp.where(degree >= order, values, jnp.zeros_like(values))

        @pl.when(step < n1)
        def _():
            for kk in range(kb):
                for q in range(n_pieces):
                    base = sc_ref[1 + q] * time_dev
                    for c in range(2):
                        for p in range(nb // 2):
                            even = r_refs[q][2 * p, c, kk]
                            odd = r_refs[q][2 * p + 1, c, kk]
                            for lo in range(2):
                                at = pl.multiple_of(c * time_all + base + lo * hi_n, hi_n)
                                if lo == 0:
                                    v = jnp.where(low, even, swap_halves(odd))
                                else:
                                    v = jnp.where(low, swap_halves(even), odd)
                                r_scr[kk, pl.ds(at, hi_n), p * LANES : (p + 1) * LANES] = v
                k = step * kb + kk
                y = lax.dot_general(
                    masked(kk, k), r_scr[kk], (((1,), (1,)), ((), ())), preferred_element_type=F32
                )
                for c in range(2):
                    at = pl.multiple_of((k * 2 + c) * pitch, 8)
                    c_ref[pl.ds(at, deg_dev), :] = y[:, c * time_all : (c + 1) * time_all]

        @pl.when((step >= n1) & (step < n1 + n2))
        def _():
            for i in range(lb):
                at = (step - n1) * lb + i
                v = c_ref[pl.ds(at, 2 * chunk_n, stride=pitch), :].astype(BF)
                w = tmp_ref[i]
                c_ref[pl.ds(at, 2 * chunk_n, stride=pitch), :] = jnp.dot(
                    v, w, preferred_element_type=F32
                )

        @pl.when(step >= n1 + n2)
        def _():
            for kk in range(kb):
                k = (step - n1 - n2) * kb + kk
                m = masked(kk, k)
                for c in range(2):
                    at = pl.multiple_of((k * 2 + c) * pitch, 8)
                    v = c_ref[pl.ds(at, deg_dev), :].astype(BF)
                    g_scr[kk, c * time_all : (c + 1) * time_all, :] = lax.dot_general(
                        v, m, (((0,), (0,)), ((), ())), preferred_element_type=F32
                    ).astype(BF)
                for q in range(n_pieces):
                    base = sc_ref[1 + n_pieces + q] * time_dev
                    out = out_refs[q]
                    for c in range(2):
                        for p in range(nb // 2):
                            at = pl.multiple_of(c * time_all + base, hi_n)
                            lanes = slice(p * LANES, (p + 1) * LANES)
                            v0 = g_scr[kk, pl.ds(at, hi_n), lanes]
                            v1 = g_scr[kk, pl.ds(at + hi_n, hi_n), lanes]
                            out[2 * p, c, kk] = jnp.where(low, v0, swap_halves(v1))
                            out[2 * p + 1, c, kk] = jnp.where(low, swap_halves(v0), v1)

    def leg_spec(kk):
        def index(s, sc):
            step = jnp.where(s < n1, s, jnp.where(s < n1 + n2, n1 - 1, s - n1 - n2))
            return (sc[row_at + step * kb + kk], 0, 0)

        return pl.BlockSpec((1, deg_dev, lat_all), index)

    piece = (nb, 2, chunk_n, hi_n, LANES)
    out_block = pl.BlockSpec(
        (nb, 2, kb, hi_n, LANES),
        lambda s, sc: (0, 0, jnp.maximum(s - n1 - n2, 0), 0, 0),
    )
    out_shape = jax.ShapeDtypeStruct(piece, BF)
    flops = 4 * chunk_n * deg_dev * lat_all * rows + 2 * deg_dev * 2 * chunk_n * time_all**2
    return pl.pallas_call(
        kernel,
        out_shape=(out_shape,) * n_pieces,
        grid_spec=pltpu.PrefetchScalarGridSpec(
            num_scalar_prefetch=1,
            grid=(n1 + n2 + n1,),
            in_specs=[leg_spec(kk) for kk in range(kb)]
            + [
                pl.BlockSpec(
                    (lb, time_all, time_all),
                    lambda s, sc: (jnp.clip(s - n1, 0, n2 - 1), 0, 0),
                ),
            ]
            + [
                pl.BlockSpec(
                    (nb, 2, kb, hi_n, LANES),
                    lambda s, sc: (0, 0, jnp.minimum(s, n1 - 1), 0, 0),
                )
            ]
            * n_pieces,
            out_specs=(out_block,) * n_pieces,
            scratch_shapes=[
                pltpu.VMEM((2 * chunk_n * pitch, time_all), F32),
                pltpu.VMEM((kb, rows, lat_all), BF),
                pltpu.VMEM((kb, rows, lat_all), BF),
            ],
        ),
        compiler_params=pltpu.CompilerParams(vmem_limit_bytes=60 << 20),
        cost_estimate=pl.CostEstimate(
            flops=flops,
            bytes_accessed=4 * chunk_n * deg_dev * lat_all
            + temporal.size * 2
            + 4 * n_pieces * gathered[0].size,
            transcendentals=0,
        ),
        name="degrees",
    )(scalars, *[legendre] * kb, temporal, *gathered)


def synthesis_call(received, tables, previous, fields, scale):
    n_tab = len(received)
    cols, hi_n, _ = received[0].shape
    length = tables[0].shape[-1]
    lo_n = 2
    cycles = LANES // lo_n
    sub = 8
    jb = 512
    batch = 4
    last = previous is not None
    n_grid = 4 if last else 2

    def kernel(*refs):
        rec_refs = refs[:n_tab]
        tab_refs = refs[n_tab : 2 * n_tab]
        grid_refs = refs[2 * n_tab : 2 * n_tab + n_grid]
        o_ref = refs[2 * n_tab + n_grid]
        sum_ref = refs[2 * n_tab + n_grid + 1] if last else None
        s_ref = refs[-1]
        h, j = pl.program_id(0), pl.program_id(1)
        if last:
            p_ref = o_ref.at[h, j]
            near_refs = refs[2 * n_tab + n_grid + 2 : 2 * n_tab + n_grid + 5]
            d_ref, r_ref = (ref.at[h, j] for ref in near_refs[:2])
            sem = refs[-2]

            def fetch(n, hh, jj):
                source = grid_refs[1 + n].at[
                    :, :, hh * sub : (hh + 1) * sub, jj * jb : (jj + 1) * jb
                ]
                return pltpu.make_async_copy(source, near_refs[n].at[hh, jj], sem.at[n, hh, jj])

            spots = [(hh, jj) for hh in range(hi_n // sub) for jj in range(length // jb)]

            @pl.when((h == 0) & (j == 0))
            def _():
                for n in (0, 1):
                    fetch(n, 0, 0).start()
                for spot in spots[1:]:
                    for n in (0, 1):
                        fetch(n, *spot).start()
                for spot in spots:
                    fetch(2, *spot).start()
        else:
            p_ref = refs[-2]

        @pl.when((h == 0) & (j == 0))
        def _():
            for n in range(n_tab):
                s_ref[n * cols * hi_n : (n + 1) * cols * hi_n, :] = (
                    rec_refs[n][...].astype(F32).reshape(cols * hi_n, LANES)
                )
            if last:
                sum_ref[...] = jnp.zeros_like(sum_ref)

        def some(i, carry):
            y = None
            for n in range(n_tab):
                parts = []
                for ii in range(batch):
                    at = n * cols * hi_n + h * sub + i * batch + ii
                    parts.append(s_ref[pl.ds(at, cols, stride=hi_n), :].astype(BF))
                term = lax.dot_general(
                    jnp.concatenate(parts, axis=1),
                    tab_refs[n][...],
                    (((0,), (0,)), ((), ())),
                    preferred_element_type=F32,
                )
                y = term if y is None else y + term
            y = y * scale
            for ii in range(batch):
                for lo in range(lo_n):
                    at = pl.ds(lo * sub + i * batch + ii, cycles, stride=lo_n * sub)
                    rows = slice((ii * lo_n + lo) * cycles, (ii * lo_n + lo + 1) * cycles)
                    for part in range(jb // LANES):
                        lanes = slice(part * LANES, (part + 1) * LANES)
                        p_ref[part, at, :] = y[rows, lanes]
            return carry

        lax.fori_loop(0, sub // batch, some, 0)
        if last:
            for hh, jj in spots:

                @pl.when((h == hh) & (j == jj))
                def _():
                    for n in (0, 1):
                        fetch(n, hh, jj).wait()

            @pl.when((h == spots[-1][0]) & (j == spots[-1][1]))
            def _():
                for spot in spots:
                    fetch(2, *spot).wait()

        group = 8

        def finish(i, carry):
            carry = list(carry)
            block = pl.ds(i * group, group)
            for part in range(jb // LANES):
                lanes = slice(part * LANES, (part + 1) * LANES)
                span = group * lo_n * sub
                rows = pl.ds(pl.multiple_of(i * span, span), span)
                p = p_ref[part, rows, :].reshape(group, lo_n, sub, LANES)
                if last:
                    p = p + grid_refs[0][block, :, :, lanes]
                    d = d_ref[block, :, :, lanes]
                    r = r_ref[block, :, :, lanes]
                    for n, term in enumerate((r * r, d * p, r * p, p * p)):
                        carry[n] = carry[n] + jnp.sum(term, axis=(0, 1))
                    p_ref[part, rows, :] = p.reshape(span, LANES)
                else:
                    p = p + grid_refs[0][block, :, :, lanes] * grid_refs[1][block, :, :, lanes]
                    o_ref[block, :, :, lanes] = p
            return tuple(carry)

        zero = (jnp.zeros((sub, LANES), F32),) * 4
        sums = lax.fori_loop(0, cycles // group, finish, zero)
        if last:
            for n in range(4):
                sum_ref[n : n + 1, :] = sum_ref[n : n + 1, :] + jnp.sum(
                    sums[n], axis=0, keepdims=True
                )

    grid_block = pl.BlockSpec((cycles, lo_n, sub, jb), lambda h, j: (0, 0, h, j))
    in_specs = (
        [pl.BlockSpec((cols, hi_n, LANES), lambda h, j: (0, 0, 0))] * n_tab
        + [pl.BlockSpec((cols, jb), lambda h, j: (0, j))] * n_tab
        + ([grid_block] + [pl.BlockSpec(memory_space=pltpu.HBM)] * 3 if last else [grid_block] * 2)
    )
    tile_rows = cycles * lo_n * sub
    if last:
        held = pltpu.VMEM((hi_n // sub, length // jb, jb // LANES, tile_rows, LANES), F32)
        whole = pl.BlockSpec(memory_space=pltpu.VMEM)
        steps = (hi_n // sub, length // jb)
        near = pltpu.VMEM(steps + (cycles, lo_n, sub, jb), F32)
        out_shape = [held, jax.ShapeDtypeStruct((sub, LANES), F32)] + [near] * 3
        out_specs = [whole, pl.BlockSpec((sub, LANES), lambda h, j: (0, 0))] + [whole] * 3
    else:
        out_shape = [jax.ShapeDtypeStruct((cycles, lo_n, hi_n, length), F32)]
        out_specs = [grid_block]
    grids = ((previous,) if last else ()) + tuple(fields)
    return pl.pallas_call(
        kernel,
        out_shape=tuple(out_shape),
        grid=(hi_n // sub, length // jb),
        in_specs=in_specs,
        out_specs=tuple(out_specs),
        scratch_shapes=[
            pltpu.SemaphoreType.DMA((3, hi_n // sub, length // jb))
            if last
            else pltpu.VMEM((jb // LANES, tile_rows, LANES), F32)
        ]
        + [pltpu.VMEM((n_tab * cols * hi_n, LANES), F32)],
        compiler_params=pltpu.CompilerParams(vmem_limit_bytes=(16 << 20) if last else (60 << 20)),
        cost_estimate=pl.CostEstimate(
            flops=2 * n_tab * cols * LANES * hi_n * length,
            bytes_accessed=4 * cycles * lo_n * hi_n * length * (n_grid + 1),
            transcendentals=0,
        ),
        name="synthesis",
    )(*received, *tables, *grids)


def update_call(sums, held):
    steps_h, steps_j, cycles, lo_n, sub, jb = held[1].shape
    parts = jb // LANES
    shape4 = (cycles, lo_n, steps_h * sub, steps_j * jb)
    group = 8
    span = group * lo_n * sub

    n_sums = len(sums)

    def kernel(*refs):
        p_ref, d_ref, r_ref, x_ref, xo_ref, ro_ref, do_ref = refs[n_sums:]
        h, j = pl.program_id(0), pl.program_id(1)
        total = refs[0][...]
        for ref in refs[1:n_sums]:
            total = total + ref[...]
        norm_now, curvature, cross, square = (
            jnp.sum(total[n : n + 1], keepdims=True) for n in range(4)
        )
        step = norm_now / curvature
        norm_next = norm_now - 2.0 * (step * cross) + step * (step * square)
        ratio = norm_next / norm_now

        def some(i, carry):
            block = pl.ds(i * group, group)
            rows = pl.ds(pl.multiple_of(i * span, span), span)
            for part in range(parts):
                lanes = slice(part * LANES, (part + 1) * LANES)
                p = p_ref[h, j, part, rows, :].reshape(group, lo_n, sub, LANES)
                d, r, x = (ref[h, j, block, :, :, lanes] for ref in (d_ref, r_ref, x_ref))
                xo_ref[block, :, :, lanes] = x + step * d
                r = r - step * p
                ro_ref[block, :, :, lanes] = r
                do_ref[block, :, :, lanes] = r + ratio * d
            return carry

        lax.fori_loop(0, cycles // group, some, 0)

    spec = pl.BlockSpec((cycles, lo_n, sub, jb), lambda h, j: (0, 0, h, j))
    size = math.prod(shape4)
    return pl.pallas_call(
        kernel,
        out_shape=(jax.ShapeDtypeStruct(shape4, F32),) * 3,
        grid=(steps_h, steps_j),
        in_specs=[pl.BlockSpec(sums[0].shape, lambda h, j: (0, 0))] * n_sums
        + [pl.BlockSpec(memory_space=pltpu.VMEM)] * 4,
        out_specs=(spec,) * 3,
        compiler_params=pltpu.CompilerParams(vmem_limit_bytes=16 << 20),
        cost_estimate=pl.CostEstimate(
            flops=6 * size, bytes_accessed=12 * size, transcendentals=0
        ),
        name="update",
    )(*sums, *(pltpu.with_memory_space_constraint(v, pltpu.VMEM) for v in held))


def add_call(values):
    def kernel(*refs):
        total = refs[0][...]
        for ref in refs[1:-1]:
            total = total + ref[...]
        refs[-1][...] = total

    return pl.pallas_call(
        kernel,
        out_shape=jax.ShapeDtypeStruct(values[0].shape, F32),
        compiler_params=pltpu.CompilerParams(vmem_limit_bytes=1 << 20),
        name="add",
    )(*values)


def sum_parts(values, n_blk, n_x, n_core):
    def stage(v, axes, perms):
        return [v] + [lax.ppermute(v, axes, perm) for perm in perms]

    n_tm = n_x * n_core
    tm = [[(i, (i + s) % n_tm) for i in range(n_tm)] for s in range(1, n_tm)]
    pair = [[(i, i ^ 1) for i in range(n_blk)]]
    rest = [[(i, (i + s) % n_blk) for i in range(n_blk)] for s in range(2, n_blk, 2)]
    values = add_call(stage(values, ("x", "core"), tm))
    values = add_call(stage(values, "blk", pair))
    return stage(values, "blk", rest)


def sine_table(phases, length):
    folded = jnp.abs(phases - length // 2) - length // 4
    x = folded.astype(F32) * (2.0 * math.pi / length)
    z = x * x
    value = jnp.full_like(z, -1.0 / math.factorial(11))
    for n in (9, 7, 5, 3, 1):
        value = value * z + (1.0 if n % 4 == 1 else -1.0) / math.factorial(n)
    return value * x


def fast_body(mesh, solution, residual, direction, noise_var, legendre, temporal, order_table):
    per_device, deg_dev, _ = legendre.shape
    cycles, time_dev, longitude = direction.shape
    nb, n_x, n_core = (mesh.shape[name] for name in ("blk", "x", "core"))
    lo_n = LANES // cycles
    hi_n = time_dev // lo_n
    chunk_n = per_device // CHUNKS
    cols = nb * 2 * chunk_n
    blk_i, x_i, core_i = (lax.axis_index(name) for name in ("blk", "x", "core"))
    half = per_device // 2
    halves_of = order_table.reshape(nb, 2, half)
    grouped = jnp.stack([jnp.min(halves_of, axis=1), jnp.max(halves_of, axis=1)])
    own = lax.dynamic_slice_in_dim(halves_of, blk_i, 1)[0]
    slots = jnp.arange(half, dtype=jnp.int32)
    flip = jnp.where(own[0] < own[1], 0, half)
    own_rows = jnp.stack([slots + flip, slots + half - flip])
    own_orders = jnp.stack([jnp.min(own, axis=0), jnp.max(own, axis=0)])
    shape4 = (cycles, lo_n, hi_n, longitude)
    fields = (solution, residual, direction, noise_var)
    solution4, residual4, direction4, noise4 = (v.reshape(shape4) for v in fields)
    quarter = (longitude // 4) * 3

    def table_of(chunk, grouped):
        high, start = PLAN[chunk]
        orders = grouped[high][:, start * chunk_n : (start + 1) * chunk_n]
        points = jnp.arange(longitude, dtype=jnp.int32)
        turn = jnp.arange(2, dtype=jnp.int32) * quarter
        phases = orders[:, None, :, None] * points + turn[None, :, None, None]
        whole = longitude & (longitude - 1) == 0
        phases = phases & (longitude - 1) if whole else phases % longitude
        return sine_table(phases, longitude).astype(BF).reshape(cols, longitude)

    forth = [jnp.mod(x_i - s, n_x) * n_core + (core_i + o) % n_core for o in range(2) for s in range(n_x)]
    back = [jnp.mod(x_i + s, n_x) * n_core + (core_i + o) % n_core for o in range(2) for s in range(n_x)]
    base = (x_i * n_core + core_i) * deg_dev
    header = jnp.stack([base] + forth + back).astype(jnp.int32)
    swap = [(i, (i + 1) % n_core) for i in range(n_core)]

    def shift(v, s, keep):
        pairs = [(i, (i + s) % n_x) for i in range(n_x)]
        return lax.ppermute(v, "x", [pair for pair in pairs if keep(*pair)])

    def across(v):
        return lax.all_to_all(v, "blk", split_axis=0, concat_axis=0, tiled=True)

    tables = [table_of(0, grouped)]
    spectra = list(analysis_call(direction4, tables, (1,), nb))
    piece = (nb, 2, chunk_n, hi_n, LANES)
    later, spectra[0] = lax.optimization_barrier((grouped, spectra[0]))
    tables += [table_of(g, later) for g in range(1, CHUNKS)]
    counts = tuple(len(trip) for trip in TRIPS[1:])
    spectra += list(analysis_call(direction4, tables[1:], counts, nb))
    temporal_narrow = temporal.astype(BF)
    arrived = []
    for n, trip in enumerate(TRIPS):
        moved = across(spectra[n])
        arrived += [moved[:, slot].reshape(piece) for slot in range(len(trip))]
    received = []
    for g, (high, start) in enumerate(PLAN):

        def forward(source, target):
            return target > 0 or not high

        def backward(source, target):
            return source > 0 or not high

        mine = arrived[g]
        own = [mine] + [shift(mine, s, forward) for s in range(1, n_x)]
        pieces = own + [lax.ppermute(v, "core", swap) for v in own]
        span = slice(start * chunk_n, (start + 1) * chunk_n)
        scalars = jnp.concatenate([header, own_orders[high, span], own_rows[high, span]])
        out = degree_call(scalars, legendre, temporal_narrow, pieces)
        keep, send = out[:n_x], out[n_x:]
        other = [lax.ppermute(send[s], "core", swap) for s in range(1, n_x)]
        halves = [
            (keep[s].astype(F32) + other[s - 1].astype(F32)).astype(BF) for s in range(1, n_x)
        ]
        parts = [shift(halves[s - 1], s, backward) for s in range(1, n_x)]
        near = lax.ppermute(send[0], "core", swap)
        total = keep[0].astype(F32) + near.astype(F32)
        for part in parts:
            total = total + part.astype(F32)
        total = total.astype(BF)
        received.append(across(total).reshape(cols, hi_n, LANES))
    scale = 2.0 / longitude
    (partial,) = synthesis_call(received[:-1], tables[:-1], None, (noise4, direction4), scale)
    product, sums, *near = synthesis_call(
        received[-1:], tables[-1:], partial, (direction4, residual4, solution4), scale
    )
    sums = sum_parts(sums, nb, n_x, n_core)
    out = update_call(sums, (product, *near))
    return tuple(v.reshape(direction.shape) for v in out)


def solution(mesh):
    n_core = 2 if mesh.shape["tm"] % 2 == 0 else 1
    n_x = mesh.shape["tm"] // n_core
    nb = mesh.shape["blk"]
    inner = Mesh(mesh.devices.reshape(nb, n_x, n_core), ("blk", "x", "core"))
    tm = ("x", "core")

    def body(*args):
        direction, legendre = args[2], args[4]
        cycles, time_dev, longitude = direction.shape
        fits = (
            n_core == 2
            and n_x == 2
            and 2 * cycles == LANES
            and time_dev == 2 * PACK
            and nb % 2 == 0
            and longitude % 512 == 0
            and legendre.shape[0] % (8 * CHUNKS) == 0
            and legendre.shape[1] % PACK == 0
            and legendre.shape[2] % LANES == 0
            and args[5].shape[-1] % LANES == 0
        )
        if fits:
            return fast_body(inner, *args)
        return plain_body(*args)

    grid = P("blk", tm, None)
    return jax.shard_map(
        body,
        mesh=inner,
        in_specs=(grid, grid, grid, grid, grid, P(tm, None, None), P()),
        out_specs=(grid, grid, grid),
        check_vma=False,
    )
```
